256 devices in a mesh: pipe: 2 (over z_lo), ctx: 64 (over z_hi, x, y), tp: 2 (over core).
Axes of the slice: x: 4, y: 4, z: 8 (z_hi: 4, z_lo: 2; z = z_hi * 2 + z_lo), core: 2. Of those that a mesh axis runs over, the one named last changes fastest.
Arguments:
- lin_query: bfloat16 [9216, 4096], P('ctx', 'tp'), may hold values from -6 to 6
- lin_key: bfloat16 [9216, 4096], P('ctx', 'tp'), may hold values from -6 to 6
- lin_value: bfloat16 [9216, 4096], P('ctx', 'tp'), may hold values from -128 to 128
- log_decay: float32 [32, 9216], P('tp', 'ctx'), may hold values from -1 to 0
- out_gate: bfloat16 [9216, 4096], P('ctx', 'tp'), may hold values from -6 to 6
- norm_gain: float32 [4096], P('tp'), may hold values from 0.1 to 1.9
- value_proj: bfloat16 [4, 1024, 128], P('tp'), may hold values from -0.1875 to 0.1875
- soft_query: bfloat16 [9216, 4096], P('ctx', 'tp'), may hold values from -16 to 16
- soft_key: bfloat16 [9216, 512], P('ctx', 'tp'), may hold values from -16 to 16
- doc_lengths: int32 [8], replicated, may hold values from 1 to 6912, 9216 in all
Outputs:
- section_out: bfloat16 [2, 9216, 4096], P('pipe', 'ctx', 'tp')
The draws below stay inside these ranges and needn't reach their ends.
Inputs may be any that keep to these rules, and one draw needn't show every extreme that they name: `doc_lengths`: they sum to 9216.
All inputs are finite; a program needn't handle non-finite values.
Results may differ from the reference program's by a relative error of at most 0.0028.
The reference program's roundings to bfloat16 on the way count: a program that leaves them out, or rounds other values in their place, can miss the bound.
Values may be sent and summed in bfloat16 or wider, within the bound.
A program may use at most 192 MiB of HBM per device.

```python
import math
import jax
import jax.numpy as jnp
import numpy as np
from jax import lax

HEADS = 32
KV_HEADS = 4
HEAD_DIM = 128
GROUP = 8
LEN_DEV = 144
SEQUENCE_LENGTH = 9216
DOCS = 8


def draw_lin_value(key, part):
    base_key = jax.random.fold_in(key, 0)
    head_frac = jnp.arange(HEADS, dtype=jnp.float32) / max(HEADS - 1, 1)
    base = jax.random.truncated_normal(base_key, -6.0, 6.0, (SEQUENCE_LENGTH, HEADS, HEAD_DIM), jnp.float32)
    head_scale = 3.0 ** head_frac
    drawn = base * head_scale[None, :, None]
    return drawn.reshape(SEQUENCE_LENGTH, HEADS * HEAD_DIM).astype(jnp.bfloat16)


def draw_log_decay(key, part):
    random_keys_divided = jax.random.split(key, 7)
    slow_share = 0.5
    slow_heads = jax.random.bernoulli(random_keys_divided[0], slow_share, (HEADS, 1))
    slow_rate = jnp.exp(jax.random.uniform(random_keys_divided[1], (HEADS, 1), jnp.float32, math.log(0.02 / SEQUENCE_LENGTH), math.log(0.2 / SEQUENCE_LENGTH)))
    fast_rate = jnp.exp(jax.random.uniform(random_keys_divided[2], (HEADS, 1), jnp.float32, math.log(1.0 / SEQUENCE_LENGTH), math.log(1.0 / 30.0)))
    head_decay_rate = jnp.where(slow_heads, slow_rate, fast_rate)
    blocks = SEQUENCE_LENGTH // LEN_DEV
    block_multiplier = jnp.exp(jax.random.uniform(random_keys_divided[3], (HEADS, blocks, 1), jnp.float32, math.log(0.5), math.log(2.0)))
    block_multiplier = jnp.broadcast_to(block_multiplier, (HEADS, blocks, LEN_DEV)).reshape(HEADS, SEQUENCE_LENGTH)
    jaggedness_level = jax.random.uniform(random_keys_divided[4], (HEADS, SEQUENCE_LENGTH), jnp.float32, 0.5, 1.5)
    spike_rows = jax.random.randint(random_keys_divided[5], (3,), 1, SEQUENCE_LENGTH)
    token_positions = jnp.arange(SEQUENCE_LENGTH)
    spike_events = jnp.any(token_positions[:, None] == spike_rows[None, :], axis=1)
    spike_keep_flags = jax.random.uniform(random_keys_divided[6], (SEQUENCE_LENGTH,), jnp.float32, 0.5, 0.8)
    spike_term = jnp.where(spike_events, jnp.log(spike_keep_flags), 0.0)
    return (-head_decay_rate * block_multiplier * jaggedness_level + spike_term[None, :]).astype(jnp.float32)


def attention_pair(key):
    random_keys_divided = jax.random.split(jax.random.fold_in(key, 11), 3)
    query = jax.random.truncated_normal(random_keys_divided[0], -6.0, 6.0, (SEQUENCE_LENGTH, HEADS, HEAD_DIM), jnp.float32)
    keyed = jax.random.truncated_normal(random_keys_divided[2], -6.0, 6.0, (SEQUENCE_LENGTH, KV_HEADS, HEAD_DIM), jnp.float32)
    return (query.reshape(SEQUENCE_LENGTH, HEADS * HEAD_DIM), keyed.reshape(SEQUENCE_LENGTH, KV_HEADS * HEAD_DIM))


def draw_soft_query(key, part):
    query, _ = attention_pair(key)
    return query.astype(jnp.bfloat16)


def draw_soft_key(key, part):
    _, keyed = attention_pair(key)
    return keyed.astype(jnp.bfloat16)


def shard_levels(rng, extent, pieces, smallest, high):
    factor_of = 1.0
    for axis_at, shards_of in pieces:
        draws = jax.random.uniform(jax.random.fold_in(jax.random.fold_in(rng, 6), axis_at), (shards_of,), jnp.float32, smallest / len(pieces), high / len(pieces))
        factor_of = factor_of * jnp.repeat(jnp.exp(draws), extent[axis_at] // shards_of).reshape((-1,) + (1,) * (len(extent) - 1 - axis_at))
    return factor_of


def profile(number_of, total, most, skew):
    weights = [(1 << 20) // math.isqrt(grade ** skew) + 1 for grade in range(2, number_of + 1)]
    spare, given = total - most - (number_of - 1), [1] * (number_of - 1)
    while spare > 0:
        free = [i for i in range(number_of - 1) if given[i] < most]
        pool, remaining = sum([weights[i] for i in free]), spare
        for i in free:
            addition = min(most - given[i], max(1, remaining * weights[i] // pool), spare)
            given[i] = given[i] + addition
            spare = spare - addition
    return np.array([most] + given)


def ragged_sizes(key, amount, total, bound, slope):
    if amount == 2:
        one = jax.random.randint(key, (), max(1, total - bound), min(bound, total - 1) + 1)
        return jnp.stack([one, total - one])
    tallies = jnp.asarray(profile(amount, total, bound, slope), jnp.int32)
    twos = (amount - 1) // 2
    donor, receiver = tallies[1:1 + 2 * twos:2], tallies[2:2 + 2 * twos:2]
    slack = jnp.minimum(donor - 1, bound - receiver)
    shifted = jax.random.randint(jax.random.fold_in(key, 1), (twos,), 0, 1 << 20) % (slack + 1)
    tallies = tallies.at[1:1 + 2 * twos:2].set(donor - shifted).at[2:2 + 2 * twos:2].set(receiver + shifted)
    return tallies[jax.random.permutation(jax.random.fold_in(key, 2), amount)]


def bell_draw(own_key, dims, deviation, limit, cuts=(), held_as=jnp.bfloat16):
    values = deviation * jax.random.normal(own_key, dims, jnp.float32)
    if cuts:
        values = values * shard_levels(own_key, dims, cuts, -0.22, 0.18)
    return jnp.clip(values, -limit, limit).astype(held_as)


def setup_inputs(seed: int = 0) -> dict:
    streams_of = jax.random.split(jax.random.key(seed), 11)
    return {
        "lin_query": bell_draw(streams_of[0], (SEQUENCE_LENGTH, HEADS * HEAD_DIM), 1.0, 6.0, ((0, 64), (1, 2))),
        "lin_key": bell_draw(streams_of[1], (SEQUENCE_LENGTH, HEADS * HEAD_DIM), 1.0, 6.0, ((0, 64), (1, 2))),
        "lin_value": draw_lin_value(jax.random.fold_in(streams_of[10], 71), 0),
        "log_decay": draw_log_decay(jax.random.fold_in(streams_of[10], 71), 0),
        "out_gate": bell_draw(streams_of[4], (SEQUENCE_LENGTH, HEADS * HEAD_DIM), 1.0, 6.0, ((0, 64), (1, 2))),
        "norm_gain": jnp.clip(1.0 + 0.18 * jax.random.normal(streams_of[5], (HEADS * HEAD_DIM,), jnp.float32), 0.1, 1.9),
        "value_proj": bell_draw(streams_of[6], (KV_HEADS, GROUP * HEAD_DIM, HEAD_DIM), (GROUP * HEAD_DIM) ** -0.5, 0.1875, ((0, 2),)),
        "soft_query": draw_soft_query(jax.random.fold_in(streams_of[10], 71), 0),
        "soft_key": draw_soft_key(jax.random.fold_in(streams_of[10], 71), 0),
        "doc_lengths": ragged_sizes(streams_of[9], DOCS, SEQUENCE_LENGTH, (3 * SEQUENCE_LENGTH) // 4, 2).astype(jnp.int32),
    }


def rounded(values_in):
    return lax.optimization_barrier(values_in.astype(jnp.bfloat16)).astype(jnp.float32)

def doc_numbers(doc_lengths, token_positions):
    doc_ends = jnp.cumsum(doc_lengths).astype(jnp.int32)
    return lax.optimization_barrier(jnp.sum((doc_ends[None, :] <= token_positions[:, None]).astype(jnp.int32), axis=1)).astype(jnp.int32)

def lightning_block(incoming, inputs):
    query_block, key_block, value_block, decay_block, doc_block, prev_doc = inputs
    row_count = query_block.shape[0]
    order = jnp.arange(row_count, dtype=jnp.int32)
    lower_mask = order[:, None] >= order[None, :]
    cum_decay = jnp.cumsum(decay_block, axis=1)
    same_doc = lower_mask & (doc_block[:, None] == doc_block[None, :])
    queries = query_block.astype(jnp.float32)
    key_rows = key_block.astype(jnp.float32)
    value_rows = value_block.astype(jnp.float32)
    scores = jnp.einsum('thd,shd->hts', queries, key_rows)
    log_gap = jnp.minimum(cum_decay[:, :, None] - cum_decay[:, None, :], 0.0)
    decay_matrix = jnp.where(same_doc[None], jnp.exp(log_gap), 0.0)
    weights = rounded(scores * decay_matrix)
    local_term = jnp.einsum('hts,shd->thd', weights, value_rows)
    continues = (doc_block == prev_doc).astype(jnp.float32)
    entry_weight = jnp.exp(cum_decay).T * continues[:, None]
    carried_term = jnp.einsum('thd,hde->the', queries, incoming, precision=lax.Precision.HIGHEST) * entry_weight[:, :, None]
    last_cum = cum_decay[:, -1]
    tail_weight = jnp.exp(last_cum[:, None] - cum_decay) * (doc_block == doc_block[-1]).astype(jnp.float32)[None, :]
    block_state = jnp.einsum('shd,she->hde', key_rows * tail_weight.T[:, :, None], value_rows, precision=lax.Precision.HIGHEST)
    carry_factor = jnp.exp(last_cum) * (doc_block[-1] == prev_doc).astype(jnp.float32)
    next_state = carry_factor[:, None, None] * incoming + block_state
    return (next_state, local_term + carried_term)

def reference(lin_query, lin_key, lin_value, log_decay, out_gate, norm_gain, value_proj, soft_query, soft_key, doc_lengths):
    blocks = SEQUENCE_LENGTH // LEN_DEV
    features = HEADS * HEAD_DIM
    token_positions = jnp.arange(SEQUENCE_LENGTH, dtype=jnp.int32)
    doc_ids = doc_numbers(doc_lengths, token_positions)
    shifted_docs = jnp.concatenate([jnp.full((1,), -1, jnp.int32), doc_ids[:-1]])
    prev_docs = shifted_docs.reshape(blocks, LEN_DEV)[:, 0]
    query_blocks = lin_query.reshape(blocks, LEN_DEV, HEADS, HEAD_DIM)
    key_blocks = lin_key.reshape(blocks, LEN_DEV, HEADS, HEAD_DIM)
    value_blocks = lin_value.reshape(blocks, LEN_DEV, HEADS, HEAD_DIM)
    decay_blocks = log_decay.reshape(HEADS, blocks, LEN_DEV).transpose(1, 0, 2)
    doc_blocks = doc_ids.reshape(blocks, LEN_DEV)
    initial = jnp.zeros((HEADS, HEAD_DIM, HEAD_DIM), jnp.float32)
    _, attention = lax.scan(lightning_block, initial, (query_blocks, key_blocks, value_blocks, decay_blocks, doc_blocks, prev_docs))
    attention = attention.reshape(SEQUENCE_LENGTH, features)
    mean_square = lax.optimization_barrier(jnp.mean(attention * attention, axis=1, keepdims=True))
    lin_out = (attention * lax.rsqrt(mean_square + 1e-06) * norm_gain[None, :] * jax.nn.sigmoid(out_gate.astype(jnp.float32))).astype(jnp.bfloat16)
    grouped = lax.optimization_barrier(lin_out).astype(jnp.float32).reshape(SEQUENCE_LENGTH, KV_HEADS, GROUP * HEAD_DIM)
    values = jnp.einsum('tgf,gfe->tge', grouped, value_proj.astype(jnp.float32))
    values = rounded(values)
    query_grid = soft_query.astype(jnp.float32).reshape(SEQUENCE_LENGTH, KV_HEADS, GROUP, HEAD_DIM)
    key_grid = soft_key.astype(jnp.float32).reshape(SEQUENCE_LENGTH, KV_HEADS, HEAD_DIM)
    scale = 1.0 / jnp.sqrt(jnp.float32(HEAD_DIM))

    def softmax_block(block_index):
        first_pos = (block_index * LEN_DEV).astype(jnp.int32)
        query_block = lax.dynamic_slice_in_dim(query_grid, first_pos, LEN_DEV, 0)
        query_docs = lax.dynamic_slice_in_dim(doc_ids, first_pos, LEN_DEV, 0)
        query_pos = first_pos + jnp.arange(LEN_DEV, dtype=jnp.int32)
        scores = jnp.einsum('tgcd,sgd->gcts', query_block, key_grid) * scale
        allowed = (token_positions[None, :] <= query_pos[:, None]) & (doc_ids[None, :] == query_docs[:, None])
        masked = jnp.where(allowed, scores, -1e+30)
        top_score = lax.optimization_barrier(jnp.max(masked, axis=-1))
        probs = jnp.where(allowed, jnp.exp(scores - top_score[..., None]), 0.0)
        denom = lax.optimization_barrier(jnp.sum(probs, axis=-1))
        numer = jnp.einsum('gcts,sgd->gctd', rounded(probs), values)
        result = numer / denom[..., None]
        return result.transpose(2, 0, 1, 3).reshape(LEN_DEV, features).astype(jnp.bfloat16)
    soft_out = lax.map(softmax_block, jnp.arange(blocks, dtype=jnp.int32)).reshape(SEQUENCE_LENGTH, features)
    return jnp.stack([lin_out, soft_out])
```

```python
import math

import jax
import jax.numpy as jnp
from jax import lax
from jax.experimental import pallas as pl
from jax.experimental.pallas import tpu as pltpu
from jax.sharding import PartitionSpec as P

MESH = pl.DeviceIdType.MESH
ALL_HEADS = 32
DIM = 128
ROWS = 144
HEADS = 8
WIDTH = HEADS * DIM
DOCS = 8
EPSILON = 1e-06
F32 = jnp.float32
BF16 = jnp.bfloat16


def place():
    ctx = lax.axis_index("ctx")
    return (
        lax.axis_index("pipe"),
        lax.div(ctx, 16),
        lax.rem(lax.div(ctx, 4), 4),
        lax.rem(ctx, 4),
        lax.axis_index("tp"),
    )


def doc_starts(docs, positions):
    end = jnp.int32(0)
    start = jnp.zeros_like(positions)
    for i in range(DOCS):
        end = end + docs[i]
        start = jnp.where(end <= positions, end, start)
    return start


def halves(x):
    high = x.astype(BF16)
    return high, (x - high.astype(F32)).astype(BF16)


def thirds(x):
    high = x.astype(BF16)
    rest = x - high.astype(F32)
    mid = rest.astype(BF16)
    return high, mid, (rest - mid.astype(F32)).astype(BF16)


def matmul(a, b, ca, cb):
    return lax.dot_general(a, b, (((ca,), (cb,)), ((), ())), preferred_element_type=F32)


def section_kernel(
    lq, lk, lv, ld, og, gain, vp, sk, docs,
    lin_out, kall, vall,
    qb, kb, vb, ldb, ogb, gb, vpb,
    bst, ybuf, ypre, yfac, tsend, xbuf, xpre, xfac, zsend, zbuf, xsend, xin, ysend, yin,
    loc, sqb,
    load_sem, ksend, krecv, vsend, vrecv, ssend, srecv, qsend, qrecv,
):
    p, z, x, y, t = place()
    ctx = z * 16 + x * 4 + y
    first = ctx * ROWS

    columns = pl.ds(pl.multiple_of(p * WIDTH, WIDTH), WIDTH)
    loads = [
        pltpu.make_async_copy(src, dst, load_sem.at[i])
        for i, (src, dst) in enumerate((
            (sk.at[:, pl.ds(pl.multiple_of(p * DIM, DIM), DIM)], kall.at[z, x, y]),
            (ld.at[pl.ds(pl.multiple_of(p * HEADS, HEADS), HEADS)], ldb),
            (lk.at[:, columns], kb),
            (lv.at[:, columns], vb),
            (lq.at[:, columns], qb),
            (og.at[:, columns], ogb),
            (gain.at[:, columns], gb),
            (vp.at[p], vpb),
        ))
    ]
    for load in loads:
        load.start()

    def y_peer(d):
        return (p, z * 16 + x * 4 + lax.rem(y + d, 4), t)

    def x_peer(d):
        return (p, z * 16 + lax.rem(x + d, 4) * 4 + y, t)

    def z_peer(d):
        return (p, lax.rem(z + d, 4) * 16 + x * 4 + y, t)

    quad = [(1 - p, ctx, t), (p, ctx, 1 - t), (1 - p, ctx, 1 - t)]

    barrier = pltpu.get_barrier_semaphore()
    for d in (1, 2, 3):
        for peer in (y_peer(d), x_peer(d), z_peer(d), quad[d - 1]):
            pl.semaphore_signal(barrier, inc=1, device_id=peer, device_id_type=MESH)
    pl.semaphore_wait(barrier, 12)

    def remote(src, dst, send, recv, i, peer):
        return pltpu.make_async_remote_copy(
            src_ref=src, dst_ref=dst, send_sem=send.at[i], recv_sem=recv.at[i],
            device_id=peer, device_id_type=MESH,
        )

    started = []

    def start(copies):
        for copy in copies:
            copy.start()
        started.extend(copies)
        return copies

    def arrived(copies):
        for copy in copies:
            copy.wait_recv()

    def gather_z(buf, send, recv):
        mine = buf.at[z, x, y]
        return start([remote(mine, mine, send, recv, d - 1, z_peer(d)) for d in (1, 2, 3)])

    def gather_x(buf, send, recv):
        mine = buf.at[:, x, y]
        return start([remote(mine, mine, send, recv, d + 2, x_peer(d)) for d in (1, 2, 3)])

    def gather_y(buf, send, recv):
        mine = buf.at[:, :, y]
        return start([remote(mine, mine, send, recv, d + 5, y_peer(d)) for d in (1, 2, 3)])

    loads[0].wait()
    phase_k = gather_z(kall, ksend, krecv)

    row = lax.broadcasted_iota(jnp.int32, (ROWS, ROWS), 0)
    col = lax.broadcasted_iota(jnp.int32, (ROWS, ROWS), 1)
    begin = doc_starts(docs, first + lax.broadcasted_iota(jnp.int32, (ROWS, 1), 0)) - first
    last_begin = doc_starts(docs, jnp.full((1, 1), first + ROWS - 1, jnp.int32)) - first
    lower = (row >= col).astype(F32).astype(BF16)
    same_doc = (row >= col) & (col >= begin)
    continues = (begin < 0).astype(F32)
    last_continues = (last_begin < 0).astype(F32)
    in_last = (lax.broadcasted_iota(jnp.int32, (ROWS, 1), 0) >= last_begin).astype(F32)

    loads[1].wait()
    pieces = thirds(ldb[...])
    cum_row = sum(matmul(a, lower, 1, 1) for a in pieces)
    cum_col = sum(matmul(lower, a, 1, 1) for a in pieces)

    loads[2].wait()
    loads[3].wait()
    for h in range(HEADS):
        cols = slice(h * DIM, (h + 1) * DIM)
        last = cum_row[h : h + 1, ROWS - 1 : ROWS]
        tail = jnp.exp(last - cum_col[:, h : h + 1]) * in_last
        parts = halves(vb[:, cols].astype(F32) * tail)
        state = matmul(kb[:, cols], jnp.concatenate(parts, axis=1), 0, 0)
        bst[h, 0:DIM, :] = state[:, :DIM] + state[:, DIM:]
        bst[h, DIM : DIM + 8, :] = jnp.broadcast_to(jnp.exp(last) * last_continues, (8, DIM))

    phase = start([
        remote(bst.at[pl.ds(2 * lax.rem(y + d, 4), 2)], ybuf.at[y], ssend, srecv, d - 1, y_peer(d))
        for d in (1, 2, 3)
    ])
    ybuf[y] = bst[pl.ds(2 * y, 2)]

    arrived(phase_k)
    phase_k = gather_x(kall, ksend, krecv)

    loads[4].wait()
    for h in range(HEADS):
        cols = slice(h * DIM, (h + 1) * DIM)
        scores = matmul(qb[:, cols], kb[:, cols], 1, 1)
        gap = jnp.minimum(cum_col[:, h : h + 1] - cum_row[h : h + 1, :], 0.0)
        weights = (scores * jnp.where(same_doc, jnp.exp(gap), 0.0)).astype(BF16)
        loc[:, cols] = matmul(weights, vb[:, cols], 1, 0)

    arrived(phase)
    for i in range(2):
        prefix = jnp.zeros((DIM, DIM), F32)
        factor = jnp.ones((8, DIM), F32)
        for k in range(4):
            ypre[k, i] = prefix
            yfac[k, i] = factor
            f = ybuf[k, i, DIM : DIM + 8, :]
            prefix = prefix * f[0:1] + ybuf[k, i, 0:DIM, :]
            factor = factor * f
        tsend[2 * i, 0:64] = prefix[0:64]
        tsend[2 * i + 1, 0:64] = prefix[64:128]
        tsend[2 * i, 64:72] = factor
        tsend[2 * i + 1, 64:72] = factor

    phase = start([
        remote(tsend.at[lax.rem(x + d, 4)], xbuf.at[x], ssend, srecv, d + 2, x_peer(d))
        for d in (1, 2, 3)
    ])
    xbuf[x] = tsend[x]
    arrived(phase)
    prefix = jnp.zeros((64, DIM), F32)
    factor = jnp.ones((8, DIM), F32)
    for k in range(4):
        xpre[k] = prefix
        xfac[k] = factor
        f = xbuf[k, 64:72, :]
        prefix = prefix * f[0:1] + xbuf[k, 0:64, :]
        factor = factor * f
    zsend[0:64] = prefix
    zsend[64:72] = factor

    phase = start([
        remote(zsend, zbuf.at[z], ssend, srecv, d + 5, z_peer(d)) for d in (1, 2, 3)
    ])
    zbuf[z] = zsend[...]
    arrived(phase_k)
    phase_k = gather_y(kall, ksend, krecv)
    arrived(phase)
    state = jnp.zeros((64, DIM), F32)
    for k in range(3):
        state = jnp.where(k < z, state * zbuf[k, 64:65, :] + zbuf[k, 0:64, :], state)
    for k in range(4):
        xsend[k] = state * xfac[k, 0:1] + xpre[k]

    phase = start([
        remote(xsend.at[lax.rem(x + d, 4)], xin.at[x], ssend, srecv, d + 8, x_peer(d))
        for d in (1, 2, 3)
    ])
    xin[x] = xsend[x]
    arrived(phase)
    for i in range(2):
        for half in range(2):
            state = xin[2 * i + half]
            span = slice(half * 64, half * 64 + 64)
            for k in range(4):
                ysend[k, i, span] = state * yfac[k, i, 0:1] + ypre[k, i, span]

    phase = start([
        remote(ysend.at[lax.rem(y + d, 4)], yin.at[y], ssend, srecv, d + 11, y_peer(d))
        for d in (1, 2, 3)
    ])
    yin[y] = ysend[y]
    arrived(phase)

    squares = jnp.zeros((ROWS, DIM), F32)
    for h in range(HEADS):
        cols = slice(h * DIM, (h + 1) * DIM)
        parts = halves(yin[h // 2, h % 2])
        carried = matmul(qb[:, cols], jnp.concatenate(parts, axis=1), 1, 0)
        weight = jnp.exp(cum_col[:, h : h + 1]) * continues
        attention = loc[:, cols] + weight * (carried[:, :DIM] + carried[:, DIM:])
        loc[:, cols] = attention
        squares = squares + attention * attention

    eye = row == col
    total = jnp.sum(squares, axis=1, keepdims=True)
    sqb[0] = jnp.broadcast_to(jnp.sum(jnp.where(eye, total, 0.0), axis=0, keepdims=True), (8, ROWS))
    phase = start([
        remote(sqb.at[0], sqb.at[i + 1], qsend, qrecv, i, quad[i]) for i in range(3)
    ])
    for load in loads[5:]:
        load.wait()
    arrived(phase)
    total = sqb[0, 0:1] + sqb[1, 0:1] + (sqb[2, 0:1] + sqb[3, 0:1])
    total = jnp.sum(jnp.where(eye, total, 0.0), axis=1, keepdims=True)
    scale = lax.rsqrt(total / (ALL_HEADS * DIM) + EPSILON)
    for h in range(HEADS):
        cols = slice(h * DIM, (h + 1) * DIM)
        gate = jax.nn.sigmoid(ogb[:, cols].astype(F32))
        lin_out[:, cols] = (loc[:, cols] * scale * gb[:, cols] * gate).astype(BF16)
    vall[z, x, y] = matmul(lin_out[...], vpb[...], 1, 0).astype(BF16)

    phase_v = gather_z(vall, vsend, vrecv)
    arrived(phase_k)
    arrived(phase_v)
    phase_v = gather_x(vall, vsend, vrecv)
    arrived(phase_v)
    phase_v = gather_y(vall, vsend, vrecv)
    arrived(phase_v)
    for copy in started:
        copy.wait_send()


def section(lq, lk, lv, ld, og, gain, vp, sk, docs):
    anywhere = pl.BlockSpec(memory_space=pl.ANY)
    vmem = pl.BlockSpec(memory_space=pltpu.VMEM)
    gathered = jax.ShapeDtypeStruct((4, 4, 4, ROWS, DIM), BF16)
    dma = pltpu.SemaphoreType.DMA
    return pl.pallas_call(
        section_kernel,
        out_shape=(jax.ShapeDtypeStruct((ROWS, WIDTH), BF16), gathered, gathered),
        in_specs=[anywhere] * 8 + [pl.BlockSpec(memory_space=pltpu.SMEM)],
        out_specs=(vmem, vmem, vmem),
        scratch_shapes=[
            pltpu.VMEM((ROWS, WIDTH), BF16),
            pltpu.VMEM((ROWS, WIDTH), BF16),
            pltpu.VMEM((ROWS, WIDTH), BF16),
            pltpu.VMEM((HEADS, ROWS), F32),
            pltpu.VMEM((ROWS, WIDTH), BF16),
            pltpu.VMEM((1, WIDTH), F32),
            pltpu.VMEM((WIDTH, DIM), BF16),
            pltpu.VMEM((HEADS, DIM + 8, DIM), F32),
            pltpu.VMEM((4, 2, DIM + 8, DIM), F32),
            pltpu.VMEM((4, 2, DIM, DIM), F32),
            pltpu.VMEM((4, 2, 8, DIM), F32),
            pltpu.VMEM((4, 72, DIM), F32),
            pltpu.VMEM((4, 72, DIM), F32),
            pltpu.VMEM((4, 64, DIM), F32),
            pltpu.VMEM((4, 8, DIM), F32),
            pltpu.VMEM((72, DIM), F32),
            pltpu.VMEM((4, 72, DIM), F32),
            pltpu.VMEM((4, 64, DIM), F32),
            pltpu.VMEM((4, 64, DIM), F32),
            pltpu.VMEM((4, 2, DIM, DIM), F32),
            pltpu.VMEM((4, 2, DIM, DIM), F32),
            pltpu.VMEM((ROWS, WIDTH), F32),
            pltpu.VMEM((4, 8, ROWS), F32),
            dma((8,)), dma((9,)), dma((9,)), dma((9,)), dma((9,)), dma((15,)), dma((15,)), dma((3,)), dma((3,)),
        ],
        compiler_params=pltpu.CompilerParams(
            collective_id=0, has_side_effects=True, vmem_limit_bytes=40 << 20
        ),
        name="section",
    )(lq, lk, lv, ld, og, gain, vp, sk, docs)


CHUNK = 256
BAND = 2
SLOPE = math.log2(math.e) / math.sqrt(DIM)


def softmax_kernel(sq, keys, values, docs, out, queries, top, total, accum, load_sem):
    p = lax.axis_index("pipe")
    first = lax.axis_index("ctx") * ROWS
    loads = [
        pltpu.make_async_copy(
            sq.at[:, pl.ds(pl.multiple_of(p * WIDTH + h * DIM, DIM), DIM)],
            queries.at[h // BAND, pl.ds((h % BAND) * ROWS, ROWS)],
            load_sem.at[h],
        )
        for h in range(HEADS)
    ]
    for load in loads:
        load.start()
    start = jnp.int32(0)
    latest = jnp.int32(0)
    end = jnp.int32(0)
    for i in range(DOCS):
        end = end + docs[i]
        start = jnp.where(end <= first, end, start)
        latest = jnp.where(end <= first + ROWS - 1, end, latest)
    begin_chunk = lax.div(start, CHUNK)
    end_chunk = lax.div(first + ROWS - 1, CHUNK) + 1
    full_from = jnp.minimum(lax.div(latest + CHUNK - 1, CHUNK), end_chunk)
    full_to = jnp.maximum(lax.div(first + 1, CHUNK), full_from)
    row = lax.rem(lax.broadcasted_iota(jnp.int32, (BAND * ROWS, 1), 0), ROWS) + first
    begin = doc_starts(docs, row)
    for load in loads:
        load.wait()
    top[...] = jnp.full_like(top, -1e30)
    total[...] = jnp.zeros_like(total)
    accum[...] = jnp.zeros_like(accum)

    def score(band, chunk, masked):
        at = pl.multiple_of(chunk * CHUNK, CHUNK)
        scores = matmul(queries[band], keys[pl.ds(at, CHUNK)], 1, 1)
        if masked:
            position = at + lax.broadcasted_iota(jnp.int32, (1, CHUNK), 1)
            scores = jnp.where((position <= row) & (position >= begin), scores, -1e30)
        return scores

    def fold(s, op):
        parts = [s[:, i : i + DIM] for i in range(0, CHUNK, DIM)]
        while len(parts) > 1:
            parts = [op(a, b) for a, b in zip(parts[::2], parts[1::2])]
        return parts[0]

    def find(chunk, masked):
        for band in range(HEADS // BAND):
            top[band] = jnp.maximum(top[band], fold(score(band, chunk, masked), jnp.maximum))

    def add(chunk, masked):
        at = pl.multiple_of(chunk * CHUNK, CHUNK)
        for band in range(HEADS // BAND):
            scores = score(band, chunk, masked)
            probs = jnp.exp2((scores - top[band][:, 0:1]) * SLOPE)
            total[band] += fold(probs, jnp.add)
            accum[band] += matmul(probs.astype(BF16), values[pl.ds(at, CHUNK)], 1, 0)

    def over(step):
        for low, high, masked in (
            (begin_chunk, full_from, True),
            (full_from, full_to, False),
            (full_to, end_chunk, True),
        ):
            @pl.loop(jnp.int32(low), jnp.int32(high))
            def _(chunk):
                step(chunk, masked)

    over(find)
    for band in range(HEADS // BAND):
        top[band] = jnp.broadcast_to(
            jnp.max(top[band], axis=1, keepdims=True), (BAND * ROWS, DIM)
        )
    over(add)
    for h in range(HEADS):
        rows = slice((h % BAND) * ROWS, (h % BAND + 1) * ROWS)
        denom = jnp.sum(total[h // BAND, rows], axis=1, keepdims=True)
        out[:, h * DIM : (h + 1) * DIM] = (accum[h // BAND, rows] / denom).astype(BF16)


def softmax(sq, keys, values, docs):
    vmem = pl.BlockSpec(memory_space=pltpu.VMEM)
    bands = HEADS // BAND
    return pl.pallas_call(
        softmax_kernel,
        out_shape=jax.ShapeDtypeStruct((ROWS, WIDTH), BF16),
        in_specs=[pl.BlockSpec(memory_space=pl.ANY), vmem, vmem, pl.BlockSpec(memory_space=pltpu.SMEM)],
        out_specs=vmem,
        scratch_shapes=[
            pltpu.VMEM((bands, BAND * ROWS, DIM), BF16),
            pltpu.VMEM((bands, BAND * ROWS, DIM), F32),
            pltpu.VMEM((bands, BAND * ROWS, DIM), F32),
            pltpu.VMEM((bands, BAND * ROWS, DIM), F32),
            pltpu.SemaphoreType.DMA((HEADS,)),
        ],
        compiler_params=pltpu.CompilerParams(vmem_limit_bytes=40 << 20),
        name="softmax",
    )(sq, keys, values, docs)


def join_kernel(lin, soft, out, mine, sems):
    p = lax.axis_index("pipe")
    peer = (1 - p, lax.axis_index("ctx"), lax.axis_index("tp"))
    barrier = pltpu.get_barrier_semaphore()
    pl.semaphore_signal(barrier, inc=1, device_id=peer, device_id_type=MESH)
    mine[...] = jnp.where(p == 0, soft[...], lin[...])
    columns = pl.ds(pl.multiple_of(p * WIDTH, WIDTH), WIDTH)
    pl.semaphore_wait(barrier, 1)
    copy = pltpu.make_async_remote_copy(
        src_ref=mine, dst_ref=out.at[0, :, columns], send_sem=sems.at[0], recv_sem=sems.at[1],
        device_id=peer, device_id_type=MESH,
    )
    copy.start()
    out[0, :, columns] = jnp.where(p == 0, lin[...], soft[...])
    copy.wait()


def join(lin, soft):
    vmem = pl.BlockSpec(memory_space=pltpu.VMEM)
    return pl.pallas_call(
        join_kernel,
        out_shape=jax.ShapeDtypeStruct((1, ROWS, 2 * WIDTH), BF16),
        in_specs=[vmem, vmem],
        out_specs=vmem,
        scratch_shapes=[pltpu.VMEM((ROWS, WIDTH), BF16), pltpu.SemaphoreType.DMA((2,))],
        compiler_params=pltpu.CompilerParams(collective_id=1, has_side_effects=True),
        name="join",
    )(lin, soft)


def local(lq, lk, lv, ld, og, gain, vp, sq, sk, docs):
    lin, keys, values = section(lq, lk, lv, ld, og, gain.reshape(1, -1), vp, sk, docs)
    soft = softmax(sq, keys.reshape(-1, DIM), values.reshape(-1, DIM), docs)
    return join(lin, soft)


def solution(mesh):
    return jax.shard_map(
        local,
        mesh=mesh,
        in_specs=(
            P("ctx", "tp"), P("ctx", "tp"), P("ctx", "tp"), P("tp", "ctx"), P("ctx", "tp"),
            P("tp"), P("tp", None, None), P("ctx", "tp"), P("ctx", "tp"), P(),
        ),
        out_specs=P("pipe", "ctx", "tp"),
        check_vma=False,
    )
```

```python
import math

import jax
import jax.numpy as jnp
from jax import lax
from jax.experimental import pallas as pl
from jax.experimental.pallas import tpu as pltpu
from jax.sharding import PartitionSpec as P

MESH = pl.DeviceIdType.MESH
ALL_HEADS = 32
DIM = 128
ROWS = 144
HEADS = 8
WIDTH = HEADS * DIM
PLANE = 16
SLICE = 64
SPAN = 8 * ROWS
GROUPS = 8
PAIRS = HEADS // 2
FAR = -(2.0**100)
SLOPE = math.log2(math.e) / math.sqrt(DIM)
DOCS = 8
EPSILON = 1e-06
F32 = jnp.float32
BF16 = jnp.bfloat16


def place():
    ctx = lax.axis_index("ctx")
    return (
        lax.axis_index("pipe"),
        lax.div(ctx, 16),
        lax.rem(lax.div(ctx, 4), 4),
        lax.rem(ctx, 4),
        lax.axis_index("tp"),
    )


def doc_starts(docs, positions):
    end = jnp.int32(0)
    start = jnp.zeros_like(positions)
    for i in range(DOCS):
        end = end + docs[i]
        start = jnp.where(end <= positions, end, start)
    return start


def halves(x):
    high = x.astype(BF16)
    return high, (x - high.astype(F32)).astype(BF16)


def thirds(x):
    high = x.astype(BF16)
    rest = x - high.astype(F32)
    mid = rest.astype(BF16)
    return high, mid, (rest - mid.astype(F32)).astype(BF16)


def matmul(a, b, ca, cb):
    return lax.dot_general(a, b, (((ca,), (cb,)), ((), ())), preferred_element_type=F32)


def section_kernel(
    lq, lk, lv, ld, og, gain, vp, sq, sk, docs,
    out,
    qb, kb, vb, ldb, ogb, gb, vpb, qs, kall, vall, tags,
    bst, pbuf, ppre, pfac, zsend, zbuf, psend, yin,
    loc, sqb, linb, softb, probs, mtab, ltab,
    load_sem, qload_sem, ksend, krecv, vsend, vrecv, ssend, srecv, zs, zr, rsend, rrecv, qsend, qrecv, osend, orecv,
):
    p, z, x, y, t = place()
    spot = x * 4 + y
    ctx = z * PLANE + spot
    first = ctx * ROWS

    columns = pl.ds(pl.multiple_of(p * WIDTH, WIDTH), WIDTH)
    loads = [
        pltpu.make_async_copy(src, dst, load_sem.at[i])
        for i, (src, dst) in enumerate((
            (sk.at[:, pl.ds(pl.multiple_of(p * DIM, DIM), DIM)], kall.at[z, x, y]),
            (ld.at[pl.ds(pl.multiple_of(p * HEADS, HEADS), HEADS)], ldb),
            (lk.at[:, columns], kb),
            (lv.at[:, columns], vb),
            (lq.at[:, columns], qb),
            (og.at[:, columns], ogb),
            (gain.at[:, columns], gb),
            (vp.at[p], vpb),
        ))
    ]
    loads += [
        pltpu.make_async_copy(
            sq.at[:, pl.ds(pl.multiple_of(p * WIDTH + h * DIM, DIM), DIM)], qs.at[h], qload_sem.at[h]
        )
        for h in range(HEADS)
    ]
    for load in loads:
        load.start()

    def plane_peer(d):
        return (p, z * PLANE + lax.rem(spot + d, PLANE), t)

    def y_peer(d):
        return (p, z * PLANE + x * 4 + lax.rem(y + d, 4), t)

    def x_peer(d):
        return (p, z * PLANE + lax.rem(x + d, 4) * 4 + y, t)

    def z_peer(d):
        return (p, lax.rem(z + d, 4) * PLANE + spot, t)

    quad = [(1 - p, ctx, t), (p, ctx, 1 - t), (1 - p, ctx, 1 - t)]

    barrier = pltpu.get_barrier_semaphore()
    for peer in [plane_peer(d) for d in range(1, PLANE)] + [z_peer(d) for d in (1, 2, 3)] + quad:
        pl.semaphore_signal(barrier, inc=1, device_id=peer, device_id_type=MESH)

    row = lax.broadcasted_iota(jnp.int32, (ROWS, ROWS), 0)
    col = lax.broadcasted_iota(jnp.int32, (ROWS, ROWS), 1)
    position = first + lax.broadcasted_iota(jnp.int32, (ROWS, 1), 0)
    begin = doc_starts(docs, position) - first
    last_begin = doc_starts(docs, jnp.full((1, 1), first + ROWS - 1, jnp.int32)) - first
    lower = (row >= col).astype(F32).astype(BF16)
    same_doc = (row >= col) & (col >= begin)
    continues = (begin < 0).astype(F32)
    last_continues = (last_begin < 0).astype(F32)
    in_last = (lax.broadcasted_iota(jnp.int32, (ROWS, 1), 0) >= last_begin).astype(F32)

    loads[0].wait()
    pl.semaphore_wait(barrier, PLANE - 1 + 6)

    def remote(src, dst, send, recv, i, peer):
        return pltpu.make_async_remote_copy(
            src_ref=src, dst_ref=dst, send_sem=send.at[i], recv_sem=recv.at[i],
            device_id=peer, device_id_type=MESH,
        )

    started = []

    def start(copies):
        for copy in copies:
            copy.start()
        started.extend(copies)
        return copies

    def arrived(copies):
        for copy in copies:
            copy.wait_recv()

    near, far = pl.ds(0, 2), pl.ds(2, 2)

    def gather_1(buf, send, recv):
        mine = buf.at[z, x, y]
        return start([remote(mine, mine, send, recv, d - 1, z_peer(d)) for d in (1, 2, 3)])

    def gather_2(buf, send, recv):
        a, b = buf.at[near, x, y], buf.at[far, x, y]
        return start(
            [remote(a, a, send, recv, d + 2, x_peer(d)) for d in (1, 2, 3)]
            + [remote(b, b, send, recv, d + 5, y_peer(d)) for d in (1, 2, 3)]
        )

    def gather_3(buf, send, recv):
        a, b = buf.at[near, :, y], buf.at[far, x]
        return start(
            [remote(a, a, send, recv, d + 8, y_peer(d)) for d in (1, 2, 3)]
            + [remote(b, b, send, recv, d + 11, x_peer(d)) for d in (1, 2, 3)]
        )

    phase_k = gather_1(kall, ksend, krecv)

    loads[1].wait()
    pieces = thirds(ldb[...])
    cum_row = sum(matmul(a, lower, 1, 1) for a in pieces)
    cum_col = sum(matmul(lower, a, 1, 1) for a in pieces)

    loads[2].wait()
    loads[3].wait()
    for h in range(HEADS):
        cols = slice(h * DIM, (h + 1) * DIM)
        last = cum_row[h : h + 1, ROWS - 1 : ROWS]
        tail = jnp.exp(last - cum_col[:, h : h + 1]) * in_last
        parts = halves(vb[:, cols].astype(F32) * tail)
        state = matmul(kb[:, cols], jnp.concatenate(parts, axis=1), 0, 0)
        state = state[:, :DIM] + state[:, DIM:]
        factor = jnp.broadcast_to(jnp.exp(last) * last_continues, (8, DIM))
        for i in range(2):
            bst[2 * h + i, 0:SLICE] = state[i * SLICE : (i + 1) * SLICE]
            bst[2 * h + i, SLICE : SLICE + 8] = factor

    phase = start([
        remote(bst.at[lax.rem(spot + d, PLANE)], pbuf.at[spot], ssend, srecv, d - 1, plane_peer(d))
        for d in range(1, PLANE)
    ])
    pbuf[spot] = bst[spot]

    arrived(phase_k)
    phase_k = gather_2(kall, ksend, krecv)

    loads[4].wait()
    for h in range(HEADS):
        cols = slice(h * DIM, (h + 1) * DIM)
        scores = matmul(qb[:, cols], kb[:, cols], 1, 1)
        gap = jnp.minimum(cum_col[:, h : h + 1] - cum_row[h : h + 1, :], 0.0)
        weights = (scores * jnp.where(same_doc, jnp.exp(gap), 0.0)).astype(BF16)
        loc[:, cols] = matmul(weights, vb[:, cols], 1, 0)

    arrived(phase)
    prefix = jnp.zeros((SLICE, DIM), F32)
    factor = jnp.ones((8, DIM), F32)
    for k in range(PLANE):
        ppre[k] = prefix
        pfac[k] = factor
        f = pbuf[k, SLICE : SLICE + 8]
        prefix = prefix * f[0:1] + pbuf[k, 0:SLICE]
        factor = factor * f
    zsend[0:SLICE] = prefix
    zsend[SLICE : SLICE + 8] = factor
    phase = start([remote(zsend, zbuf.at[z], zs, zr, d - 1, z_peer(d)) for d in (1, 2, 3)])
    zbuf[z] = zsend[...]

    arrived(phase_k)
    phase_k = gather_3(kall, ksend, krecv)

    lane = lax.broadcasted_iota(jnp.int32, (1, DIM), 1)
    low = jnp.full((1, DIM), 2 * ALL_HEADS * SPAN, jnp.int32)
    high = jnp.zeros((1, DIM), jnp.int32)
    end = jnp.int32(0)
    for i in range(DOCS):
        low = jnp.where(lane == i, end, low)
        end = end + docs[i]
        high = jnp.where(lane == i, end, high)

    @pl.loop(0, 4 * PLANE)
    def _(block):
        at = block * ROWS + lax.broadcasted_iota(jnp.int32, (ROWS, 1), 0)
        tags[block] = ((at >= low) & (at < high)).astype(F32).astype(BF16)

    other = jnp.where((position >= low) & (position < high) | (lane >= DOCS), 0.0, FAR).astype(BF16)
    for h in range(HEADS):
        mtab[h] = jnp.full((ROWS, DIM), FAR, F32)
        ltab[h] = jnp.zeros((ROWS, DIM), F32)

    arrived(phase)
    state = jnp.zeros((SLICE, DIM), F32)
    for k in range(3):
        state = jnp.where(k < z, state * zbuf[k, SLICE : SLICE + 1] + zbuf[k, 0:SLICE], state)
    for k in range(PLANE):
        psend[k] = state * pfac[k, 0:1] + ppre[k]
    phase = start([
        remote(psend.at[lax.rem(spot + d, PLANE)], yin.at[spot], rsend, rrecv, d - 1, plane_peer(d))
        for d in range(1, PLANE)
    ])
    yin[spot] = psend[spot]
    for load in loads[5:]:
        load.wait()
    arrived(phase)

    squares = jnp.zeros((ROWS, DIM), F32)
    for h in range(HEADS):
        cols = slice(h * DIM, (h + 1) * DIM)
        parts = halves(yin[2 * h : 2 * h + 2].reshape(DIM, DIM))
        carried = matmul(qb[:, cols], jnp.concatenate(parts, axis=1), 1, 0)
        weight = jnp.exp(cum_col[:, h : h + 1]) * continues
        attention = loc[:, cols] + weight * (carried[:, :DIM] + carried[:, DIM:])
        loc[:, cols] = attention
        squares = squares + attention * attention

    eye = row == col
    total = jnp.sum(squares, axis=1, keepdims=True)
    sqb[0] = jnp.broadcast_to(jnp.sum(jnp.where(eye, total, 0.0), axis=0, keepdims=True), (8, ROWS))
    phase = start([
        remote(sqb.at[0], sqb.at[i + 1], qsend, qrecv, i, quad[i]) for i in range(3)
    ])
    for h in range(HEADS):
        cols = slice(h * DIM, (h + 1) * DIM)
        gate = jax.nn.sigmoid(ogb[:, cols].astype(F32))
        loc[:, cols] = loc[:, cols] * (gb[:, cols] * gate)
    arrived(phase)
    total = sqb[0, 0:1] + sqb[1, 0:1] + (sqb[2, 0:1] + sqb[3, 0:1])
    total = jnp.sum(jnp.where(eye, total, 0.0), axis=1, keepdims=True)
    scale = lax.rsqrt(total / (ALL_HEADS * DIM) + EPSILON)
    for h in range(HEADS):
        cols = slice(h * DIM, (h + 1) * DIM)
        linb[:, cols] = (loc[:, cols] * scale).astype(BF16)
    vall[z, x, y] = matmul(linb[...], vpb[...], 1, 0).astype(BF16)
    phase_v = gather_1(vall, vsend, vrecv)

    lin_copy = remote(linb, out.at[0, :, columns], osend, orecv, 0, quad[0])

    @pl.when(p == 1)
    def _():
        lin_copy.start()

    @pl.when(p == 0)
    def _():
        out[0, :, columns] = linb[...]

    arrived(phase_k)

    def probe(group, diagonal):
        over = group // 2
        wide = pl.ds(2 * lax.rem(group, 2), 2)
        keys = jnp.concatenate(
            [
                kall[over, wide].reshape(SPAN, DIM),
                tags[pl.ds(group * 8, 8)].reshape(SPAN, DIM),
            ],
            axis=1,
        )

        @pl.loop(0, PAIRS)
        def _(pair):
            for i in range(2):
                h = 2 * pair + i
                scores = matmul(jnp.concatenate([qs[h], other], axis=1), keys, 1, 1)
                if diagonal:
                    at = group * SPAN + lax.broadcasted_iota(jnp.int32, (1, SPAN), 1)
                    scores = jnp.where(at <= position, scores, FAR)
                top = jnp.max(scores, axis=1, keepdims=True)
                prob = jnp.exp2((scores - top) * SLOPE)
                denom = jnp.sum(prob, axis=1, keepdims=True)
                probs[group, h] = prob.astype(BF16)
                mtab[h] = jnp.where(lane == group, top, mtab[h])
                ltab[h] = jnp.where(lane == group, denom, ltab[h])

    whole = lax.div(ctx, 8)
    part = lax.div(whole, 3)
    probe(whole, True)
    arrived(phase_v)
    phase_v = gather_2(vall, vsend, vrecv)

    @pl.loop(jnp.int32(0), part)
    def _(group):
        probe(group, False)

    arrived(phase_v)
    phase_v = gather_3(vall, vsend, vrecv)

    @pl.loop(part, whole)
    def _(group):
        probe(group, False)

    for h in range(HEADS):
        table = mtab[h]
        top = jnp.max(table, axis=1, keepdims=True)
        share = jnp.exp2((table - top) * SLOPE)
        denom = jnp.sum(share * ltab[h], axis=1, keepdims=True)
        mtab[h] = share
        ltab[h] = jnp.broadcast_to(denom, (ROWS, DIM))
    arrived(phase_v)

    soft_copies = [
        remote(softb.at[i], out.at[0, :, pl.ds(pl.multiple_of(p * WIDTH + 2 * i * DIM, 2 * DIM), 2 * DIM)],
               osend, orecv, i + 1, quad[0])
        for i in range(PAIRS)
    ]
    for i in range(PAIRS):
        def step(group, sums):
            values = vall[group // 2, pl.ds(2 * lax.rem(group, 2), 2)].reshape(SPAN, DIM)
            result = []
            for j in range(2):
                share = jnp.sum(jnp.where(lane == group, mtab[2 * i + j], 0.0), axis=1, keepdims=True)
                result.append(sums[j] + share * matmul(probs[group, 2 * i + j], values, 1, 0))
            return tuple(result)

        sums = lax.fori_loop(
            jnp.int32(0), whole + 1, step, (jnp.zeros((ROWS, DIM), F32), jnp.zeros((ROWS, DIM), F32))
        )
        for j in range(2):
            softb[i, :, j * DIM : (j + 1) * DIM] = (sums[j] / ltab[2 * i + j]).astype(BF16)

        @pl.when(p == 0)
        def _():
            soft_copies[i].start()

        @pl.when(p == 1)
        def _():
            out[0, :, pl.ds(pl.multiple_of(p * WIDTH + 2 * i * DIM, 2 * DIM), 2 * DIM)] = softb[i]

    for copy in started:
        copy.wait_send()

    @pl.when(p == 0)
    def _():
        for copy in soft_copies:
            copy.wait_send()
        lin_copy.wait_recv()

    @pl.when(p == 1)
    def _():
        lin_copy.wait_send()
        for copy in soft_copies:
            copy.wait_recv()


def local(lq, lk, lv, ld, og, gain, vp, sq, sk, docs):
    anywhere = pl.BlockSpec(memory_space=pl.ANY)
    vmem = pl.BlockSpec(memory_space=pltpu.VMEM)
    dma = lambda n: pltpu.SemaphoreType.DMA((n,))
    blocks = (4, 4, 4, ROWS, DIM)
    return pl.pallas_call(
        section_kernel,
        out_shape=jax.ShapeDtypeStruct((1, ROWS, 2 * WIDTH), BF16),
        in_specs=[anywhere] * 9 + [pl.BlockSpec(memory_space=pltpu.SMEM)],
        out_specs=vmem,
        scratch_shapes=[
            pltpu.VMEM((ROWS, WIDTH), BF16),
            pltpu.VMEM((ROWS, WIDTH), BF16),
            pltpu.VMEM((ROWS, WIDTH), BF16),
            pltpu.VMEM((HEADS, ROWS), F32),
            pltpu.VMEM((ROWS, WIDTH), BF16),
            pltpu.VMEM((1, WIDTH), F32),
            pltpu.VMEM((WIDTH, DIM), BF16),
            pltpu.VMEM((HEADS, ROWS, DIM), BF16),
            pltpu.VMEM(blocks, BF16),
            pltpu.VMEM(blocks, BF16),
            pltpu.VMEM((4 * PLANE, ROWS, DIM), BF16),
            pltpu.VMEM((PLANE, SLICE + 8, DIM), F32),
            pltpu.VMEM((PLANE, SLICE + 8, DIM), F32),
            pltpu.VMEM((PLANE, SLICE, DIM), F32),
            pltpu.VMEM((PLANE, 8, DIM), F32),
            pltpu.VMEM((SLICE + 8, DIM), F32),
            pltpu.VMEM((4, SLICE + 8, DIM), F32),
            pltpu.VMEM((PLANE, SLICE, DIM), F32),
            pltpu.VMEM((PLANE, SLICE, DIM), F32),
            pltpu.VMEM((ROWS, WIDTH), F32),
            pltpu.VMEM((4, 8, ROWS), F32),
            pltpu.VMEM((ROWS, WIDTH), BF16),
            pltpu.VMEM((PAIRS, ROWS, 2 * DIM), BF16),
            pltpu.VMEM((GROUPS, HEADS, ROWS, SPAN), BF16),
            pltpu.VMEM((HEADS, ROWS, DIM), F32),
            pltpu.VMEM((HEADS, ROWS, DIM), F32),
            dma(8), dma(8), dma(15), dma(15), dma(15), dma(15), dma(15), dma(15), dma(3), dma(3),
            dma(15), dma(15), dma(3), dma(3), dma(5), dma(5),
        ],
        compiler_params=pltpu.CompilerParams(
            collective_id=0, has_side_effects=True, vmem_limit_bytes=60 << 20
        ),
        name="section",
    )(lq, lk, lv, ld, og, gain.reshape(1, -1), vp, sq, sk, docs)


def solution(mesh):
    return jax.shard_map(
        local,
        mesh=mesh,
        in_specs=(
            P("ctx", "tp"), P("ctx", "tp"), P("ctx", "tp"), P("tp", "ctx"), P("ctx", "tp"),
            P("tp"), P("tp", None, None), P("ctx", "tp"), P("ctx", "tp"), P(),
        ),
        out_specs=P("pipe", "ctx", "tp"),
        check_vma=False,
    )
```

```python
import math

import jax
import jax.numpy as jnp
from jax import lax
from jax.experimental import pallas as pl
from jax.experimental.pallas import tpu as pltpu
from jax.sharding import PartitionSpec as P

MESH = pl.DeviceIdType.MESH
ALL_HEADS = 32
DIM = 128
ROWS = 144
HEADS = 8
WIDTH = HEADS * DIM
PLANE = 16
SLICE = 64
SPAN = 8 * ROWS
GROUPS = 8
TEAM = 4
TEAMS = HEADS // TEAM
FAR = -(2.0**100)
SLOPE = math.log2(math.e) / math.sqrt(DIM)
DOCS = 8
EPSILON = 1e-06
F32 = jnp.float32
BF16 = jnp.bfloat16


def place():
    ctx = lax.axis_index("ctx")
    return (
        lax.axis_index("pipe"),
        lax.div(ctx, 16),
        lax.rem(lax.div(ctx, 4), 4),
        lax.rem(ctx, 4),
        lax.axis_index("tp"),
    )


def doc_starts(docs, positions):
    end = jnp.int32(0)
    start = jnp.zeros_like(positions)
    for i in range(DOCS):
        end = end + docs[i]
        start = jnp.where(end <= positions, end, start)
    return start


def halves(x):
    high = x.astype(BF16)
    return high, (x - high.astype(F32)).astype(BF16)


def thirds(x):
    high = x.astype(BF16)
    rest = x - high.astype(F32)
    mid = rest.astype(BF16)
    return high, mid, (rest - mid.astype(F32)).astype(BF16)


def matmul(a, b, ca, cb):
    return lax.dot_general(a, b, (((ca,), (cb,)), ((), ())), preferred_element_type=F32)


def section_kernel(
    lq, lk, lv, ld, og, gain, vp, sq, sk, docs,
    out,
    qb, kb, vb, ldb, ogb, gb, vpb, qs, kall, vall, tags,
    bst, pbuf, ppre, pfac, zsend, zbuf, psend, yin,
    loc, sqb, linb, softb, probs, mtab, ltab, asum,
    load_sem, qload_sem, ksend, krecv, vsend, vrecv, ssend, srecv, zs, zr, rsend, rrecv, qsend, qrecv, osend, orecv,
):
    p, z, x, y, t = place()
    spot = x * 4 + y
    ctx = z * PLANE + spot
    first = ctx * ROWS

    columns = pl.ds(pl.multiple_of(p * WIDTH, WIDTH), WIDTH)
    loads = [
        pltpu.make_async_copy(src, dst, load_sem.at[i])
        for i, (src, dst) in enumerate((
            (sk.at[:, pl.ds(pl.multiple_of(p * DIM, DIM), DIM)], kall.at[z, x, y]),
            (ld.at[pl.ds(pl.multiple_of(p * HEADS, HEADS), HEADS)], ldb),
            (lk.at[:, columns], kb),
            (lv.at[:, columns], vb),
            (lq.at[:, columns], qb),
            (og.at[:, columns], ogb),
            (gain.at[:, columns], gb),
            (vp.at[p], vpb),
        ))
    ]
    loads += [
        pltpu.make_async_copy(
            sq.at[:, pl.ds(pl.multiple_of(p * WIDTH + h * DIM, DIM), DIM)], qs.at[h], qload_sem.at[h]
        )
        for h in range(HEADS)
    ]
    for load in loads:
        load.start()

    def plane_peer(d):
        return (p, z * PLANE + lax.rem(spot + d, PLANE), t)

    def y_peer(d):
        return (p, z * PLANE + x * 4 + lax.rem(y + d, 4), t)

    def x_peer(d):
        return (p, z * PLANE + lax.rem(x + d, 4) * 4 + y, t)

    def z_peer(d):
        return (p, lax.rem(z + d, 4) * PLANE + spot, t)

    quad = [(1 - p, ctx, t), (p, ctx, 1 - t), (1 - p, ctx, 1 - t)]

    barrier = pltpu.get_barrier_semaphore()
    for peer in [plane_peer(d) for d in range(1, PLANE)] + [z_peer(d) for d in (1, 2, 3)] + quad:
        pl.semaphore_signal(barrier, inc=1, device_id=peer, device_id_type=MESH)

    row = lax.broadcasted_iota(jnp.int32, (ROWS, ROWS), 0)
    col = lax.broadcasted_iota(jnp.int32, (ROWS, ROWS), 1)
    position = first + lax.broadcasted_iota(jnp.int32, (ROWS, 1), 0)
    begin = doc_starts(docs, position) - first
    last_begin = doc_starts(docs, jnp.full((1, 1), first + ROWS - 1, jnp.int32)) - first
    lower = (row >= col).astype(F32).astype(BF16)
    same_doc = (row >= col) & (col >= begin)
    continues = (begin < 0).astype(F32)
    last_continues = (last_begin < 0).astype(F32)
    in_last = (lax.broadcasted_iota(jnp.int32, (ROWS, 1), 0) >= last_begin).astype(F32)

    loads[0].wait()
    pl.semaphore_wait(barrier, PLANE - 1 + 6)

    def remote(src, dst, send, recv, i, peer):
        return pltpu.make_async_remote_copy(
            src_ref=src, dst_ref=dst, send_sem=send.at[i], recv_sem=recv.at[i],
            device_id=peer, device_id_type=MESH,
        )

    started = []

    def start(copies):
        for copy in copies:
            copy.start()
        started.extend(copies)
        return copies

    def arrived(copies):
        for copy in copies:
            copy.wait_recv()

    near, far = pl.ds(0, 2), pl.ds(2, 2)

    def gather_1(buf, send, recv):
        mine = buf.at[z, x, y]
        return start([remote(mine, mine, send, recv, d - 1, z_peer(d)) for d in (1, 2, 3)])

    def gather_2(buf, send, recv):
        a, b = buf.at[near, x, y], buf.at[far, x, y]
        return start(
            [remote(a, a, send, recv, d + 2, x_peer(d)) for d in (1, 2, 3)]
            + [remote(b, b, send, recv, d + 5, y_peer(d)) for d in (1, 2, 3)]
        )

    def gather_3(buf, send, recv, half):
        a, b = buf.at[half, :, y], buf.at[half + 2, x]
        return start(
            [remote(a, a, send, recv, d + 8 + 6 * half, y_peer(d)) for d in (1, 2, 3)]
            + [remote(b, b, send, recv, d + 11 + 6 * half, x_peer(d)) for d in (1, 2, 3)]
        )

    phase_k = gather_1(kall, ksend, krecv)

    loads[1].wait()
    pieces = thirds(ldb[...])
    cum_row = sum(matmul(a, lower, 1, 1) for a in pieces)
    cum_col = sum(matmul(lower, a, 1, 1) for a in pieces)

    loads[2].wait()
    loads[3].wait()
    for h in range(HEADS):
        cols = slice(h * DIM, (h + 1) * DIM)
        last = cum_row[h : h + 1, ROWS - 1 : ROWS]
        tail = jnp.exp(last - cum_col[:, h : h + 1]) * in_last
        parts = halves(vb[:, cols].astype(F32) * tail)
        state = matmul(kb[:, cols], jnp.concatenate(parts, axis=1), 0, 0)
        state = state[:, :DIM] + state[:, DIM:]
        factor = jnp.broadcast_to(jnp.exp(last) * last_continues, (8, DIM))
        for i in range(2):
            bst[2 * h + i, 0:SLICE] = state[i * SLICE : (i + 1) * SLICE]
            bst[2 * h + i, SLICE : SLICE + 8] = factor

    phase = start([
        remote(bst.at[lax.rem(spot + d, PLANE)], pbuf.at[spot], ssend, srecv, d - 1, plane_peer(d))
        for d in range(1, PLANE)
    ])
    pbuf[spot] = bst[spot]

    loads[4].wait()
    for h in range(HEADS):
        cols = slice(h * DIM, (h + 1) * DIM)
        scores = matmul(qb[:, cols], kb[:, cols], 1, 1)
        gap = jnp.minimum(cum_col[:, h : h + 1] - cum_row[h : h + 1, :], 0.0)
        weights = (scores * jnp.where(same_doc, jnp.exp(gap), 0.0)).astype(BF16)
        loc[:, cols] = matmul(weights, vb[:, cols], 1, 0)

    arrived(phase)
    prefix = jnp.zeros((SLICE, DIM), F32)
    factor = jnp.ones((8, DIM), F32)
    for k in range(PLANE):
        ppre[k] = prefix
        pfac[k] = factor
        f = pbuf[k, SLICE : SLICE + 8]
        prefix = prefix * f[0:1] + pbuf[k, 0:SLICE]
        factor = factor * f
    zsend[0:SLICE] = prefix
    zsend[SLICE : SLICE + 8] = factor
    phase = start([remote(zsend, zbuf.at[z], zs, zr, d - 1, z_peer(d)) for d in (1, 2, 3)])
    zbuf[z] = zsend[...]

    arrived(phase_k)
    phase_k = gather_2(kall, ksend, krecv)

    lane = lax.broadcasted_iota(jnp.int32, (1, DIM), 1)
    low = jnp.full((1, DIM), 2 * ALL_HEADS * SPAN, jnp.int32)
    high = jnp.zeros((1, DIM), jnp.int32)
    end = jnp.int32(0)
    for i in range(DOCS):
        low = jnp.where(lane == i, end, low)
        end = end + docs[i]
        high = jnp.where(lane == i, end, high)

    @pl.loop(0, 4 * PLANE)
    def _(block):
        at = block * ROWS + lax.broadcasted_iota(jnp.int32, (ROWS, 1), 0)
        tags[block] = ((at >= low) & (at < high)).astype(F32).astype(BF16)

    other = jnp.where((position >= low) & (position < high) | (lane >= DOCS), 0.0, FAR).astype(BF16)
    others = jnp.concatenate([other] * TEAM, axis=0)
    for h in range(HEADS):
        mtab[h] = jnp.full((ROWS, DIM), FAR, F32)
        ltab[h] = jnp.zeros((ROWS, DIM), F32)

    arrived(phase)
    state = jnp.zeros((SLICE, DIM), F32)
    for k in range(3):
        state = jnp.where(k < z, state * zbuf[k, SLICE : SLICE + 1] + zbuf[k, 0:SLICE], state)
    for k in range(PLANE):
        psend[k] = state * pfac[k, 0:1] + ppre[k]
    phase = start([
        remote(psend.at[lax.rem(spot + d, PLANE)], yin.at[spot], rsend, rrecv, d - 1, plane_peer(d))
        for d in range(1, PLANE)
    ])
    yin[spot] = psend[spot]
    for load in loads[5:]:
        load.wait()
    arrived(phase_k)
    arrived(phase)
    phase_k = [gather_3(kall, ksend, krecv, half) for half in (0, 1)]

    squares = jnp.zeros((ROWS, DIM), F32)
    for h in range(HEADS):
        cols = slice(h * DIM, (h + 1) * DIM)
        parts = halves(yin[2 * h : 2 * h + 2].reshape(DIM, DIM))
        carried = matmul(qb[:, cols], jnp.concatenate(parts, axis=1), 1, 0)
        weight = jnp.exp(cum_col[:, h : h + 1]) * continues
        attention = loc[:, cols] + weight * (carried[:, :DIM] + carried[:, DIM:])
        loc[:, cols] = attention
        squares = squares + attention * attention

    eye = row == col
    total = jnp.sum(squares, axis=1, keepdims=True)
    sqb[0] = jnp.broadcast_to(jnp.sum(jnp.where(eye, total, 0.0), axis=0, keepdims=True), (8, ROWS))
    phase = start([
        remote(sqb.at[0], sqb.at[i + 1], qsend, qrecv, i, quad[i]) for i in range(3)
    ])
    for h in range(HEADS):
        cols = slice(h * DIM, (h + 1) * DIM)
        gate = jax.nn.sigmoid(ogb[:, cols].astype(F32))
        loc[:, cols] = loc[:, cols] * (gb[:, cols] * gate)
    arrived(phase)
    total = sqb[0, 0:1] + sqb[1, 0:1] + (sqb[2, 0:1] + sqb[3, 0:1])
    total = jnp.sum(jnp.where(eye, total, 0.0), axis=1, keepdims=True)
    scale = lax.rsqrt(total / (ALL_HEADS * DIM) + EPSILON)
    for h in range(HEADS):
        cols = slice(h * DIM, (h + 1) * DIM)
        linb[:, cols] = (loc[:, cols] * scale).astype(BF16)
    vall[z, x, y] = matmul(linb[...], vpb[...], 1, 0).astype(BF16)
    phase_v = gather_1(vall, vsend, vrecv)

    @pl.when(p == 0)
    def _():
        out[0, :, columns] = linb[...]

    def probe(group, diagonal):
        over = group // 2
        wide = pl.ds(2 * lax.rem(group, 2), 2)
        keys = jnp.concatenate(
            [
                kall[over, wide].reshape(SPAN, DIM),
                tags[pl.ds(group * 8, 8)].reshape(SPAN, DIM),
            ],
            axis=1,
        )

        @pl.loop(0, TEAMS)
        def _(team):
            heads = pl.ds(team * TEAM, TEAM)
            asked = jnp.concatenate([qs[heads].reshape(TEAM * ROWS, DIM), others], axis=1)
            raw = matmul(asked, keys, 1, 1)
            for i in range(TEAM):
                h = team * TEAM + i
                scores = raw[i * ROWS : (i + 1) * ROWS]
                if diagonal:
                    at = group * SPAN + lax.broadcasted_iota(jnp.int32, (1, SPAN), 1)
                    scores = jnp.where(at <= position, scores, FAR)
                top = jnp.max(scores, axis=1, keepdims=True)
                prob = jnp.exp2((scores - top) * SLOPE)
                denom = jnp.sum(prob, axis=1, keepdims=True)
                probs[group, h] = prob.astype(BF16)
                mtab[h] = jnp.where(lane == group, top, mtab[h])
                ltab[h] = jnp.where(lane == group, denom, ltab[h])

    whole = lax.div(ctx, 8)

    def nth(half, i):
        return lax.div(i, 2) * 4 + lax.rem(i, 2) + 2 * half

    def below(half, limit):
        return sum(lax.div(limit + 7 - nth(half, jnp.int32(i)), 8) for i in range(4))

    def probe_half(half):
        @pl.loop(jnp.int32(0), below(half, whole))
        def _(i):
            probe(nth(half, i), False)

    arrived(phase_v)
    phase_v = gather_2(vall, vsend, vrecv)
    lin_copy = remote(linb, out.at[0, :, columns], osend, orecv, 0, quad[0])

    @pl.when(p == 1)
    def _():
        lin_copy.start()

    arrived(phase_k[0])
    probe_half(0)
    arrived(phase_v)
    phase_v = [gather_3(vall, vsend, vrecv, half) for half in (0, 1)]
    arrived(phase_k[1])
    probe(whole, True)
    probe_half(1)

    for h in range(HEADS):
        table = mtab[h]
        top = jnp.max(table, axis=1, keepdims=True)
        share = jnp.exp2((table - top) * SLOPE)
        denom = jnp.sum(share * ltab[h], axis=1, keepdims=True)
        mtab[h] = share
        ltab[h] = jnp.broadcast_to(denom, (ROWS, DIM))

    def gathered(half, team, sums):
        def step(n, sums):
            group = nth(half, n)
            values = vall[group // 2, pl.ds(2 * lax.rem(group, 2), 2)].reshape(SPAN, DIM)
            heads = pl.ds(team * TEAM, TEAM)
            product = matmul(probs[group, heads].reshape(TEAM * ROWS, SPAN), values, 1, 0)
            result = []
            for i in range(TEAM):
                share = jnp.sum(jnp.where(lane == group, mtab[team * TEAM + i], 0.0), axis=1, keepdims=True)
                result.append(sums[i] + share * product[i * ROWS : (i + 1) * ROWS])
            return tuple(result)

        return lax.fori_loop(jnp.int32(0), below(half, whole + 1), step, sums)

    arrived(phase_v[0])
    for team in range(TEAMS):
        sums = gathered(0, team, tuple(jnp.zeros((ROWS, DIM), F32) for _ in range(TEAM)))
        for i in range(TEAM):
            asum[team * TEAM + i] = sums[i]
    arrived(phase_v[1])

    def team_columns(team):
        return pl.ds(pl.multiple_of(p * WIDTH + team * TEAM * DIM, TEAM * DIM), TEAM * DIM)

    soft_copies = [
        remote(softb.at[team], out.at[0, :, team_columns(team)], osend, orecv, team + 1, quad[0])
        for team in range(TEAMS)
    ]
    for team in range(TEAMS):
        sums = gathered(1, team, tuple(asum[team * TEAM + i] for i in range(TEAM)))
        for i in range(TEAM):
            softb[team, :, i * DIM : (i + 1) * DIM] = (sums[i] / ltab[team * TEAM + i]).astype(BF16)

        @pl.when(p == 0)
        def _():
            soft_copies[team].start()

        @pl.when(p == 1)
        def _():
            out[0, :, team_columns(team)] = softb[team]

    for copy in started:
        copy.wait_send()

    @pl.when(p == 0)
    def _():
        for copy in soft_copies:
            copy.wait_send()
        lin_copy.wait_recv()

    @pl.when(p == 1)
    def _():
        lin_copy.wait_send()
        for copy in soft_copies:
            copy.wait_recv()


def local(lq, lk, lv, ld, og, gain, vp, sq, sk, docs):
    anywhere = pl.BlockSpec(memory_space=pl.ANY)
    vmem = pl.BlockSpec(memory_space=pltpu.VMEM)
    dma = lambda n: pltpu.SemaphoreType.DMA((n,))
    blocks = (4, 4, 4, ROWS, DIM)
    return pl.pallas_call(
        section_kernel,
        out_shape=jax.ShapeDtypeStruct((1, ROWS, 2 * WIDTH), BF16),
        in_specs=[anywhere] * 9 + [pl.BlockSpec(memory_space=pltpu.SMEM)],
        out_specs=vmem,
        scratch_shapes=[
            pltpu.VMEM((ROWS, WIDTH), BF16),
            pltpu.VMEM((ROWS, WIDTH), BF16),
            pltpu.VMEM((ROWS, WIDTH), BF16),
            pltpu.VMEM((HEADS, ROWS), F32),
            pltpu.VMEM((ROWS, WIDTH), BF16),
            pltpu.VMEM((1, WIDTH), F32),
            pltpu.VMEM((WIDTH, DIM), BF16),
            pltpu.VMEM((HEADS, ROWS, DIM), BF16),
            pltpu.VMEM(blocks, BF16),
            pltpu.VMEM(blocks, BF16),
            pltpu.VMEM((4 * PLANE, ROWS, DIM), BF16),
            pltpu.VMEM((PLANE, SLICE + 8, DIM), F32),
            pltpu.VMEM((PLANE, SLICE + 8, DIM), F32),
            pltpu.VMEM((PLANE, SLICE, DIM), F32),
            pltpu.VMEM((PLANE, 8, DIM), F32),
            pltpu.VMEM((SLICE + 8, DIM), F32),
            pltpu.VMEM((4, SLICE + 8, DIM), F32),
            pltpu.VMEM((PLANE, SLICE, DIM), F32),
            pltpu.VMEM((PLANE, SLICE, DIM), F32),
            pltpu.VMEM((ROWS, WIDTH), F32),
            pltpu.VMEM((4, 8, ROWS), F32),
            pltpu.VMEM((ROWS, WIDTH), BF16),
            pltpu.VMEM((TEAMS, ROWS, TEAM * DIM), BF16),
            pltpu.VMEM((GROUPS, HEADS, ROWS, SPAN), BF16),
            pltpu.VMEM((HEADS, ROWS, DIM), F32),
            pltpu.VMEM((HEADS, ROWS, DIM), F32),
            pltpu.VMEM((HEADS, ROWS, DIM), F32),
            dma(8), dma(8), dma(21), dma(21), dma(21), dma(21), dma(15), dma(15), dma(3), dma(3),
            dma(15), dma(15), dma(3), dma(3), dma(1 + TEAMS), dma(1 + TEAMS),
        ],
        compiler_params=pltpu.CompilerParams(
            collective_id=0, has_side_effects=True, vmem_limit_bytes=60 << 20
        ),
        name="section",
    )(lq, lk, lv, ld, og, gain.reshape(1, -1), vp, sq, sk, docs)


def solution(mesh):
    return jax.shard_map(
        local,
        mesh=mesh,
        in_specs=(
            P("ctx", "tp"), P("ctx", "tp"), P("ctx", "tp"), P("tp", "ctx"), P("ctx", "tp"),
            P("tp"), P("tp", None, None), P("ctx", "tp"), P("ctx", "tp"), P(),
        ),
        out_specs=P("pipe", "ctx", "tp"),
        check_vma=False,
    )
```

```python
import math

import jax
import jax.numpy as jnp
from jax import lax
from jax.experimental import pallas as pl
from jax.experimental.pallas import tpu as pltpu
from jax.sharding import PartitionSpec as P

MESH = pl.DeviceIdType.MESH
ALL_HEADS = 32
DIM = 128
ROWS = 144
HEADS = 8
WIDTH = HEADS * DIM
PLANE = 16
SLICE = 64
SPAN = 8 * ROWS
GROUPS = 8
TEAM = 4
TEAMS = HEADS // TEAM
PARTS = ((0, 4), (4, 4))
FAR = -(2.0**100)
SLOPE = math.log2(math.e) / math.sqrt(DIM)
DOCS = 8
EPSILON = 1e-06
F32 = jnp.float32
BF16 = jnp.bfloat16


def place():
    ctx = lax.axis_index("ctx")
    return (
        lax.axis_index("pipe"),
        lax.div(ctx, 16),
        lax.rem(lax.div(ctx, 4), 4),
        lax.rem(ctx, 4),
        lax.axis_index("tp"),
    )


def doc_starts(docs, positions):
    end = jnp.int32(0)
    start = jnp.zeros_like(positions)
    for i in range(DOCS):
        end = end + docs[i]
        start = jnp.where(end <= positions, end, start)
    return start


def halves(x):
    high = x.astype(BF16)
    return high, (x - high.astype(F32)).astype(BF16)


def thirds(x):
    high = x.astype(BF16)
    rest = x - high.astype(F32)
    mid = rest.astype(BF16)
    return high, mid, (rest - mid.astype(F32)).astype(BF16)


def matmul(a, b, ca, cb):
    return lax.dot_general(a, b, (((ca,), (cb,)), ((), ())), preferred_element_type=F32)


def section_kernel(
    lq, lk, lv, ld, og, gain, vp, sq, sk, docs,
    out,
    qb, kb, vb, ldb, ogb, gb, vpb, qs, kall, vall, tags,
    bst, pbuf, ppre, pfac, zsend, zbuf, psend, yin,
    loc, sqb, linb, softb, probs, mtab, ltab, asum,
    load_sem, qload_sem, ksend, krecv, vsend, vrecv, ssend, srecv, zs, zr, rsend, rrecv, qsend, qrecv, osend, orecv, own_sem,
):
    p, z, x, y, t = place()
    spot = x * 4 + y
    ctx = z * PLANE + spot
    first = ctx * ROWS

    columns = pl.ds(pl.multiple_of(p * WIDTH, WIDTH), WIDTH)
    loads = [
        pltpu.make_async_copy(src, dst, load_sem.at[i])
        for i, (src, dst) in enumerate((
            (sk.at[:, pl.ds(pl.multiple_of(p * DIM, DIM), DIM)], kall.at[z, x, y]),
            (ld.at[pl.ds(pl.multiple_of(p * HEADS, HEADS), HEADS)], ldb),
            (lk.at[:, columns], kb),
            (lv.at[:, columns], vb),
            (lq.at[:, columns], qb),
            (og.at[:, columns], ogb),
            (gain.at[:, columns], gb),
            (vp.at[p], vpb),
        ))
    ]
    loads += [
        pltpu.make_async_copy(
            sq.at[:, pl.ds(pl.multiple_of(p * WIDTH + h * DIM, DIM), DIM)], qs.at[h], qload_sem.at[h]
        )
        for h in range(HEADS)
    ]

    def plane_peer(d):
        return (p, z * PLANE + lax.rem(spot + d, PLANE), t)

    def y_peer(d):
        return (p, z * PLANE + x * 4 + lax.rem(y + d, 4), t)

    def x_peer(d):
        return (p, z * PLANE + lax.rem(x + d, 4) * 4 + y, t)

    def z_peer(d):
        return (p, lax.rem(z + d, 4) * PLANE + spot, t)

    quad = [(1 - p, ctx, t), (p, ctx, 1 - t), (1 - p, ctx, 1 - t)]

    barrier = pltpu.get_barrier_semaphore()
    for peer in [plane_peer(d) for d in range(1, PLANE)] + [z_peer(d) for d in (1, 2, 3)] + quad:
        pl.semaphore_signal(barrier, inc=1, device_id=peer, device_id_type=MESH)
    for load in loads:
        load.start()

    row = lax.broadcasted_iota(jnp.int32, (ROWS, ROWS), 0)
    col = lax.broadcasted_iota(jnp.int32, (ROWS, ROWS), 1)
    position = first + lax.broadcasted_iota(jnp.int32, (ROWS, 1), 0)
    begin = doc_starts(docs, position) - first
    last_begin = doc_starts(docs, jnp.full((1, 1), first + ROWS - 1, jnp.int32)) - first
    lower = (row >= col).astype(F32).astype(BF16)
    same_doc = (row >= col) & (col >= begin)
    continues = (begin < 0).astype(F32)
    last_continues = (last_begin < 0).astype(F32)
    in_last = (lax.broadcasted_iota(jnp.int32, (ROWS, 1), 0) >= last_begin).astype(F32)

    loads[0].wait()
    pl.semaphore_wait(barrier, PLANE - 1 + 6)

    def remote(src, dst, send, recv, i, peer):
        return pltpu.make_async_remote_copy(
            src_ref=src, dst_ref=dst, send_sem=send.at[i], recv_sem=recv.at[i],
            device_id=peer, device_id_type=MESH,
        )

    started = []

    def only(condition, act, copies):
        def all_of_them():
            for copy in copies:
                act(copy)

        if condition is None:
            all_of_them()
        else:
            pl.when(condition)(all_of_them)

    def start_bundles(bundles):
        for copies, sends, _ in bundles:
            only(sends, lambda copy: copy.start(), copies)
        started.extend(bundles)
        return bundles

    def start(copies):
        return start_bundles([(copies, None, None)])

    def arrived(bundles):
        for copies, _, receives in bundles:
            only(receives, lambda copy: copy.wait_recv(), copies)

    def upto(layer):
        return None if layer == 0 else z >= layer

    def gather_1(buf, send, recv):
        mine = buf.at[z, x, y]
        return start_bundles([
            ([remote(mine, mine, send, recv, d - 1, z_peer(d))], z + d < 4, z >= d) for d in (1, 2, 3)
        ])

    def gather_2(buf, send, recv):
        bundles = []
        for layer in range(4):
            mine, peer = buf.at[layer, x, y], x_peer if layer < 2 else y_peer
            copies = [remote(mine, mine, send, recv, 3 * layer + d + 2, peer(d)) for d in (1, 2, 3)]
            bundles.append((copies, upto(layer), upto(layer)))
        return start_bundles(bundles)

    def gather_3(buf, send, recv, half):
        a, b = buf.at[half, :, y], buf.at[half + 2, x]
        via_y = [remote(a, a, send, recv, d + 14 + 6 * half, y_peer(d)) for d in (1, 2, 3)]
        via_x = [remote(b, b, send, recv, d + 17 + 6 * half, x_peer(d)) for d in (1, 2, 3)]
        return start_bundles([
            (via_y, upto(half), upto(half)), (via_x, upto(half + 2), upto(half + 2)),
        ])

    phase_k = gather_1(kall, ksend, krecv)

    loads[1].wait()
    pieces = thirds(ldb[...])
    cum_row = sum(matmul(a, lower, 1, 1) for a in pieces)
    cum_col = sum(matmul(lower, a, 1, 1) for a in pieces)

    loads[2].wait()
    loads[3].wait()
    for h in range(HEADS):
        cols = slice(h * DIM, (h + 1) * DIM)
        last = cum_row[h : h + 1, ROWS - 1 : ROWS]
        tail = jnp.exp(last - cum_col[:, h : h + 1]) * in_last
        parts = halves(vb[:, cols].astype(F32) * tail)
        state = matmul(kb[:, cols], jnp.concatenate(parts, axis=1), 0, 0)
        state = state[:, :DIM] + state[:, DIM:]
        factor = jnp.broadcast_to(jnp.exp(last) * last_continues, (8, DIM))
        for i in range(2):
            bst[2 * h + i, 0:SLICE] = state[i * SLICE : (i + 1) * SLICE]
            bst[2 * h + i, SLICE : SLICE + 8] = factor

    phase = start([
        remote(bst.at[lax.rem(spot + d, PLANE)], pbuf.at[spot], ssend, srecv, d - 1, plane_peer(d))
        for d in range(1, PLANE)
    ])
    pbuf[spot] = bst[spot]

    loads[4].wait()
    for h in range(HEADS):
        cols = slice(h * DIM, (h + 1) * DIM)
        scores = matmul(qb[:, cols], kb[:, cols], 1, 1)
        gap = jnp.minimum(cum_col[:, h : h + 1] - cum_row[h : h + 1, :], 0.0)
        weights = (scores * jnp.where(same_doc, jnp.exp(gap), 0.0)).astype(BF16)
        loc[:, cols] = matmul(weights, vb[:, cols], 1, 0)

    arrived(phase)
    prefix = jnp.zeros((SLICE, DIM), F32)
    factor = jnp.ones((8, DIM), F32)
    for k in range(PLANE):
        ppre[k] = prefix
        pfac[k] = factor
        f = pbuf[k, SLICE : SLICE + 8]
        prefix = prefix * f[0:1] + pbuf[k, 0:SLICE]
        factor = factor * f
    zsend[0:SLICE] = prefix
    zsend[SLICE : SLICE + 8] = factor
    phase = start([remote(zsend, zbuf.at[z], zs, zr, d - 1, z_peer(d)) for d in (1, 2, 3)])
    zbuf[z] = zsend[...]

    arrived(phase_k)
    phase_k = gather_2(kall, ksend, krecv)

    lane = lax.broadcasted_iota(jnp.int32, (1, DIM), 1)
    low = jnp.full((1, DIM), 2 * ALL_HEADS * SPAN, jnp.int32)
    high = jnp.zeros((1, DIM), jnp.int32)
    end = jnp.int32(0)
    for i in range(DOCS):
        low = jnp.where(lane == i, end, low)
        end = end + docs[i]
        high = jnp.where(lane == i, end, high)

    @pl.loop(0, 4 * PLANE)
    def _(block):
        at = block * ROWS + lax.broadcasted_iota(jnp.int32, (ROWS, 1), 0)
        tags[block] = ((at >= low) & (at < high)).astype(F32).astype(BF16)

    other = jnp.where((position >= low) & (position < high) | (lane >= DOCS), 0.0, FAR).astype(BF16)
    others = jnp.concatenate([other] * HEADS, axis=0)
    for h in range(HEADS):
        mtab[h] = jnp.full((ROWS, DIM), FAR, F32)
        ltab[h] = jnp.zeros((ROWS, DIM), F32)

    arrived(phase)
    state = jnp.zeros((SLICE, DIM), F32)
    for k in range(3):
        state = jnp.where(k < z, state * zbuf[k, SLICE : SLICE + 1] + zbuf[k, 0:SLICE], state)
    for k in range(PLANE):
        psend[k] = state * pfac[k, 0:1] + ppre[k]
    phase = start([
        remote(psend.at[lax.rem(spot + d, PLANE)], yin.at[spot], rsend, rrecv, d - 1, plane_peer(d))
        for d in range(1, PLANE)
    ])
    yin[spot] = psend[spot]
    for load in loads[5:]:
        load.wait()
    arrived(phase_k)
    arrived(phase)
    phase_k = [gather_3(kall, ksend, krecv, half) for half in (0, 1)]

    squares = jnp.zeros((ROWS, DIM), F32)
    for h in range(HEADS):
        cols = slice(h * DIM, (h + 1) * DIM)
        parts = halves(yin[2 * h : 2 * h + 2].reshape(DIM, DIM))
        carried = matmul(qb[:, cols], jnp.concatenate(parts, axis=1), 1, 0)
        weight = jnp.exp(cum_col[:, h : h + 1]) * continues
        attention = loc[:, cols] + weight * (carried[:, :DIM] + carried[:, DIM:])
        loc[:, cols] = attention
        squares = squares + attention * attention

    eye = row == col
    total = jnp.sum(squares, axis=1, keepdims=True)
    sqb[0] = jnp.broadcast_to(jnp.sum(jnp.where(eye, total, 0.0), axis=0, keepdims=True), (8, ROWS))
    phase = start([
        remote(sqb.at[0], sqb.at[i + 1], qsend, qrecv, i, quad[i]) for i in range(3)
    ])
    for h in range(HEADS):
        cols = slice(h * DIM, (h + 1) * DIM)
        gate = jax.nn.sigmoid(ogb[:, cols].astype(F32))
        loc[:, cols] = loc[:, cols] * (gb[:, cols] * gate)
    arrived(phase)
    total = sqb[0, 0:1] + sqb[1, 0:1] + (sqb[2, 0:1] + sqb[3, 0:1])
    total = jnp.sum(jnp.where(eye, total, 0.0), axis=1, keepdims=True)
    scale = lax.rsqrt(total / (ALL_HEADS * DIM) + EPSILON)
    for h in range(HEADS):
        cols = slice(h * DIM, (h + 1) * DIM)
        linb[:, cols] = (loc[:, cols] * scale).astype(BF16)
    vall[z, x, y] = matmul(linb[...], vpb[...], 1, 0).astype(BF16)
    phase_v = gather_1(vall, vsend, vrecv)

    lin_own = pltpu.make_async_copy(linb, out.at[0, :, columns], own_sem.at[len(PARTS)])

    @pl.when(p == 0)
    def _():
        lin_own.start()

    def probe(group, diagonal):
        over = group // 2
        wide = pl.ds(2 * lax.rem(group, 2), 2)
        keys = jnp.concatenate(
            [
                kall[over, wide].reshape(SPAN, DIM),
                tags[pl.ds(group * 8, 8)].reshape(SPAN, DIM),
            ],
            axis=1,
        )

        if True:
            asked = jnp.concatenate([qs[...].reshape(HEADS * ROWS, DIM), others], axis=1)
            raw = matmul(asked, keys, 1, 1)
            for h in range(HEADS):
                i = h
                scores = raw[i * ROWS : (i + 1) * ROWS]
                if diagonal:
                    at = group * SPAN + lax.broadcasted_iota(jnp.int32, (1, SPAN), 1)
                    scores = jnp.where(at <= position, scores, FAR)
                top = jnp.max(scores, axis=1, keepdims=True)
                prob = jnp.exp2((scores - top) * SLOPE)
                denom = jnp.sum(prob, axis=1, keepdims=True)
                probs[group, h] = prob.astype(BF16)
                mtab[h] = jnp.where(lane == group, top, mtab[h])
                ltab[h] = jnp.where(lane == group, denom, ltab[h])

    whole = lax.div(ctx, 8)

    def nth(half, i):
        return lax.div(i, 2) * 4 + lax.rem(i, 2) + 2 * half

    def below(half, limit):
        return sum(lax.div(limit + 7 - nth(half, jnp.int32(i)), 8) for i in range(4))

    def probe_half(half, low, high):
        @pl.loop(low, high)
        def _(i):
            probe(nth(half, i), False)

    arrived(phase_v)
    phase_v = gather_2(vall, vsend, vrecv)
    lin_copy = remote(linb, out.at[0, :, columns], osend, orecv, 0, quad[0])

    @pl.when(p == 1)
    def _():
        lin_copy.start()

    arrived(phase_k[0])
    ready, some = below(0, whole), lax.div(below(0, whole), 2)
    probe_half(0, jnp.int32(0), some)
    arrived(phase_v)
    phase_v = [gather_3(vall, vsend, vrecv, half) for half in (0, 1)]
    probe_half(0, some, ready)
    arrived(phase_k[1])
    probe(whole, True)
    probe_half(1, jnp.int32(0), below(1, whole))

    for h in range(HEADS):
        table = mtab[h]
        top = jnp.max(table, axis=1, keepdims=True)
        share = jnp.exp2((table - top) * SLOPE)
        denom = jnp.sum(share * ltab[h], axis=1, keepdims=True)
        mtab[h] = share
        ltab[h] = jnp.broadcast_to(denom, (ROWS, DIM))

    def gathered(half, start_head, size, sums):
        def step(n, sums):
            group = nth(half, n)
            values = vall[group // 2, pl.ds(2 * lax.rem(group, 2), 2)].reshape(SPAN, DIM)
            heads = pl.ds(start_head, size)
            product = matmul(probs[group, heads].reshape(size * ROWS, SPAN), values, 1, 0)
            result = []
            for i in range(size):
                share = jnp.sum(jnp.where(lane == group, mtab[start_head + i], 0.0), axis=1, keepdims=True)
                result.append(sums[i] + share * product[i * ROWS : (i + 1) * ROWS])
            return tuple(result)

        return lax.fori_loop(jnp.int32(0), below(half, whole + 1), step, sums)

    arrived(phase_v[0])
    sums = gathered(0, 0, HEADS, tuple(jnp.zeros((ROWS, DIM), F32) for _ in range(HEADS)))
    for h in range(HEADS):
        asum[h] = sums[h]
    arrived(phase_v[1])

    def share_of(part):
        low, size = PARTS[part]
        return softb.at[:, pl.ds(low * DIM, size * DIM)], out.at[
            0, :, pl.ds(pl.multiple_of(p * WIDTH + low * DIM, 2 * DIM), size * DIM)
        ]

    soft_copies = [
        remote(*share_of(part), osend, orecv, part + 1, quad[0]) for part in range(len(PARTS))
    ]
    soft_own = [
        pltpu.make_async_copy(*share_of(part), own_sem.at[part]) for part in range(len(PARTS))
    ]
    for team, (low, size) in enumerate(PARTS):
        sums = gathered(1, low, size, tuple(asum[low + i] for i in range(size)))
        for i in range(size):
            softb[:, (low + i) * DIM : (low + i + 1) * DIM] = (sums[i] / ltab[low + i]).astype(BF16)

        @pl.when(p == 0)
        def _():
            soft_copies[team].start()

        @pl.when(p == 1)
        def _():
            soft_own[team].start()

    for copies, sends, _ in started:
        only(sends, lambda copy: copy.wait_send(), copies)

    @pl.when(p == 0)
    def _():
        for copy in soft_copies:
            copy.wait_send()
        lin_copy.wait_recv()
        lin_own.wait()

    @pl.when(p == 1)
    def _():
        lin_copy.wait_send()
        for copy in soft_own:
            copy.wait()
        for copy in soft_copies:
            copy.wait_recv()


def local(lq, lk, lv, ld, og, gain, vp, sq, sk, docs):
    anywhere = pl.BlockSpec(memory_space=pl.ANY)
    vmem = pl.BlockSpec(memory_space=pltpu.VMEM)
    dma = lambda n: pltpu.SemaphoreType.DMA((n,))
    blocks = (4, 4, 4, ROWS, DIM)
    return pl.pallas_call(
        section_kernel,
        out_shape=jax.ShapeDtypeStruct((1, ROWS, 2 * WIDTH), BF16),
        in_specs=[anywhere] * 9 + [pl.BlockSpec(memory_space=pltpu.SMEM)],
        out_specs=anywhere,
        scratch_shapes=[
            pltpu.VMEM((ROWS, WIDTH), BF16),
            pltpu.VMEM((ROWS, WIDTH), BF16),
            pltpu.VMEM((ROWS, WIDTH), BF16),
            pltpu.VMEM((HEADS, ROWS), F32),
            pltpu.VMEM((ROWS, WIDTH), BF16),
            pltpu.VMEM((1, WIDTH), F32),
            pltpu.VMEM((WIDTH, DIM), BF16),
            pltpu.VMEM((HEADS, ROWS, DIM), BF16),
            pltpu.VMEM(blocks, BF16),
            pltpu.VMEM(blocks, BF16),
            pltpu.VMEM((4 * PLANE, ROWS, DIM), BF16),
            pltpu.VMEM((PLANE, SLICE + 8, DIM), F32),
            pltpu.VMEM((PLANE, SLICE + 8, DIM), F32),
            pltpu.VMEM((PLANE, SLICE, DIM), F32),
            pltpu.VMEM((PLANE, 8, DIM), F32),
            pltpu.VMEM((SLICE + 8, DIM), F32),
            pltpu.VMEM((4, SLICE + 8, DIM), F32),
            pltpu.VMEM((PLANE, SLICE, DIM), F32),
            pltpu.VMEM((PLANE, SLICE, DIM), F32),
            pltpu.VMEM((ROWS, WIDTH), F32),
            pltpu.VMEM((4, 8, ROWS), F32),
            pltpu.VMEM((ROWS, WIDTH), BF16),
            pltpu.VMEM((ROWS, WIDTH), BF16),
            pltpu.VMEM((GROUPS, HEADS, ROWS, SPAN), BF16),
            pltpu.VMEM((HEADS, ROWS, DIM), F32),
            pltpu.VMEM((HEADS, ROWS, DIM), F32),
            pltpu.VMEM((HEADS, ROWS, DIM), F32),
            dma(8), dma(8), dma(27), dma(27), dma(27), dma(27), dma(15), dma(15), dma(3), dma(3),
            dma(15), dma(15), dma(3), dma(3), dma(1 + len(PARTS)), dma(1 + len(PARTS)), dma(1 + len(PARTS)),
        ],
        compiler_params=pltpu.CompilerParams(
            collective_id=0, has_side_effects=True, vmem_limit_bytes=60 << 20
        ),
        name="section",
    )(lq, lk, lv, ld, og, gain.reshape(1, -1), vp, sq, sk, docs)


def solution(mesh):
    return jax.shard_map(
        local,
        mesh=mesh,
        in_specs=(
            P("ctx", "tp"), P("ctx", "tp"), P("ctx", "tp"), P("tp", "ctx"), P("ctx", "tp"),
            P("tp"), P("tp", None, None), P("ctx", "tp"), P("ctx", "tp"), P(),
        ),
        out_specs=P("pipe", "ctx", "tp"),
        check_vma=False,
    )
```

```python
import math

import jax
import jax.numpy as jnp
from jax import lax
from jax.experimental import pallas as pl
from jax.experimental.pallas import tpu as pltpu
from jax.sharding import PartitionSpec as P

MESH = pl.DeviceIdType.MESH
ALL_HEADS = 32
DIM = 128
ROWS = 144
HEADS = 8
WIDTH = HEADS * DIM
PLANE = 16
SLICE = 64
SPAN = 8 * ROWS
GROUPS = 8
TEAM = 4
TEAMS = HEADS // TEAM
PARTS = ((0, 4), (4, 4))
FAR = -(2.0**100)
SLOPE = math.log2(math.e) / math.sqrt(DIM)
DOCS = 8
EPSILON = 1e-06
F32 = jnp.float32
BF16 = jnp.bfloat16


def place():
    ctx = lax.axis_index("ctx")
    return (
        lax.axis_index("pipe"),
        lax.div(ctx, 16),
        lax.rem(lax.div(ctx, 4), 4),
        lax.rem(ctx, 4),
        lax.axis_index("tp"),
    )


def doc_starts(docs, positions):
    end = jnp.int32(0)
    start = jnp.zeros_like(positions)
    for i in range(DOCS):
        end = end + docs[i]
        start = jnp.where(end <= positions, end, start)
    return start


def halves(x):
    high = x.astype(BF16)
    return high, (x - high.astype(F32)).astype(BF16)


def thirds(x):
    high = x.astype(BF16)
    rest = x - high.astype(F32)
    mid = rest.astype(BF16)
    return high, mid, (rest - mid.astype(F32)).astype(BF16)


def matmul(a, b, ca, cb):
    return lax.dot_general(a, b, (((ca,), (cb,)), ((), ())), preferred_element_type=F32)


def section_kernel(
    lq, lk, lv, ld, og, gain, vp, sq, sk, docs,
    out,
    qb, kb, vb, ldb, ogb, gb, vpb, qs, kall, vall, tags,
    bst, pbuf, ppre, pfac, zsend, zbuf, psend, yin,
    loc, sqb, linb, softb, probs, mtab, ltab, dsum, asum,
    load_sem, qload_sem, ksend, krecv, vsend, vrecv, ssend, srecv, zs, zr, rsend, rrecv, qsend, qrecv, osend, orecv, own_sem,
):
    p, z, x, y, t = place()
    spot = x * 4 + y
    ctx = z * PLANE + spot
    first = ctx * ROWS

    columns = pl.ds(pl.multiple_of(p * WIDTH, WIDTH), WIDTH)
    loads = [
        pltpu.make_async_copy(src, dst, load_sem.at[i])
        for i, (src, dst) in enumerate((
            (sk.at[:, pl.ds(pl.multiple_of(p * DIM, DIM), DIM)], kall.at[z, x, y]),
            (ld.at[pl.ds(pl.multiple_of(p * HEADS, HEADS), HEADS)], ldb),
            (lk.at[:, columns], kb),
            (lv.at[:, columns], vb),
            (lq.at[:, columns], qb),
            (og.at[:, columns], ogb),
            (gain.at[:, columns], gb),
            (vp.at[p], vpb),
        ))
    ]
    loads += [
        pltpu.make_async_copy(
            sq.at[:, pl.ds(pl.multiple_of(p * WIDTH + h * DIM, DIM), DIM)], qs.at[h], qload_sem.at[h]
        )
        for h in range(HEADS)
    ]

    def plane_peer(d):
        return (p, z * PLANE + lax.rem(spot + d, PLANE), t)

    def y_peer(d):
        return (p, z * PLANE + x * 4 + lax.rem(y + d, 4), t)

    def x_peer(d):
        return (p, z * PLANE + lax.rem(x + d, 4) * 4 + y, t)

    def z_peer(d):
        return (p, lax.rem(z + d, 4) * PLANE + spot, t)

    quad = [(1 - p, ctx, t), (p, ctx, 1 - t), (1 - p, ctx, 1 - t)]

    barrier = pltpu.get_barrier_semaphore()
    for peer in [plane_peer(d) for d in range(1, PLANE)] + [z_peer(d) for d in (1, 2, 3)] + quad:
        pl.semaphore_signal(barrier, inc=1, device_id=peer, device_id_type=MESH)
    for load in loads:
        load.start()

    row = lax.broadcasted_iota(jnp.int32, (ROWS, ROWS), 0)
    col = lax.broadcasted_iota(jnp.int32, (ROWS, ROWS), 1)
    position = first + lax.broadcasted_iota(jnp.int32, (ROWS, 1), 0)
    begin = doc_starts(docs, position) - first
    last_begin = doc_starts(docs, jnp.full((1, 1), first + ROWS - 1, jnp.int32)) - first
    lower = (row >= col).astype(F32).astype(BF16)
    same_doc = (row >= col) & (col >= begin)
    continues = (begin < 0).astype(F32)
    last_continues = (last_begin < 0).astype(F32)
    in_last = (lax.broadcasted_iota(jnp.int32, (ROWS, 1), 0) >= last_begin).astype(F32)

    loads[0].wait()
    pl.semaphore_wait(barrier, PLANE - 1 + 6)

    def remote(src, dst, send, recv, i, peer):
        return pltpu.make_async_remote_copy(
            src_ref=src, dst_ref=dst, send_sem=send.at[i], recv_sem=recv.at[i],
            device_id=peer, device_id_type=MESH,
        )

    started = []

    def only(condition, act, copies):
        def all_of_them():
            for copy in copies:
                act(copy)

        if condition is None:
            all_of_them()
        else:
            pl.when(condition)(all_of_them)

    def start_bundles(bundles):
        for copies, sends, _ in bundles:
            only(sends, lambda copy: copy.start(), copies)
        started.extend(bundles)
        return bundles

    def start(copies):
        return start_bundles([(copies, None, None)])

    def arrived(bundles):
        for copies, _, receives in bundles:
            only(receives, lambda copy: copy.wait_recv(), copies)

    def upto(layer):
        return None if layer == 0 else z >= layer

    def gather_1(buf, send, recv):
        mine = buf.at[z, x, y]
        return start_bundles([
            ([remote(mine, mine, send, recv, d - 1, z_peer(d))], z + d < 4, z >= d) for d in (1, 2, 3)
        ])

    def gather_2(buf, send, recv):
        bundles = []
        for layer in range(4):
            mine, peer = buf.at[layer, x, y], x_peer if layer < 2 else y_peer
            copies = [remote(mine, mine, send, recv, 3 * layer + d + 2, peer(d)) for d in (1, 2, 3)]
            bundles.append((copies, upto(layer), upto(layer)))
        return start_bundles(bundles)

    def gather_3(buf, send, recv, half):
        a, b = buf.at[half, :, y], buf.at[half + 2, x]
        via_y = [remote(a, a, send, recv, d + 14 + 6 * half, y_peer(d)) for d in (1, 2, 3)]
        via_x = [remote(b, b, send, recv, d + 17 + 6 * half, x_peer(d)) for d in (1, 2, 3)]
        return start_bundles([
            (via_y, upto(half), upto(half)), (via_x, upto(half + 2), upto(half + 2)),
        ])

    phase_k = gather_1(kall, ksend, krecv)

    loads[1].wait()
    pieces = thirds(ldb[...])
    cum_row = sum(matmul(a, lower, 1, 1) for a in pieces)
    cum_col = sum(matmul(lower, a, 1, 1) for a in pieces)

    loads[2].wait()
    loads[3].wait()
    for h in range(HEADS):
        cols = slice(h * DIM, (h + 1) * DIM)
        last = cum_row[h : h + 1, ROWS - 1 : ROWS]
        tail = jnp.exp(last - cum_col[:, h : h + 1]) * in_last
        parts = halves(vb[:, cols].astype(F32) * tail)
        state = matmul(kb[:, cols], jnp.concatenate(parts, axis=1), 0, 0)
        state = state[:, :DIM] + state[:, DIM:]
        factor = jnp.broadcast_to(jnp.exp(last) * last_continues, (8, DIM))
        for i in range(2):
            bst[2 * h + i, 0:SLICE] = state[i * SLICE : (i + 1) * SLICE]
            bst[2 * h + i, SLICE : SLICE + 8] = factor

    phase = start([
        remote(bst.at[lax.rem(spot + d, PLANE)], pbuf.at[spot], ssend, srecv, d - 1, plane_peer(d))
        for d in range(1, PLANE)
    ])
    pbuf[spot] = bst[spot]

    loads[4].wait()
    for h in range(HEADS):
        cols = slice(h * DIM, (h + 1) * DIM)
        scores = matmul(qb[:, cols], kb[:, cols], 1, 1)
        gap = jnp.minimum(cum_col[:, h : h + 1] - cum_row[h : h + 1, :], 0.0)
        weights = (scores * jnp.where(same_doc, jnp.exp(gap), 0.0)).astype(BF16)
        loc[:, cols] = matmul(weights, vb[:, cols], 1, 0)

    arrived(phase)
    prefix = jnp.zeros((SLICE, DIM), F32)
    factor = jnp.ones((8, DIM), F32)
    for k in range(PLANE):
        ppre[k] = prefix
        pfac[k] = factor
        f = pbuf[k, SLICE : SLICE + 8]
        prefix = prefix * f[0:1] + pbuf[k, 0:SLICE]
        factor = factor * f
    zsend[0:SLICE] = prefix
    zsend[SLICE : SLICE + 8] = factor
    phase = start([remote(zsend, zbuf.at[z], zs, zr, d - 1, z_peer(d)) for d in (1, 2, 3)])
    zbuf[z] = zsend[...]

    arrived(phase_k)
    phase_k = gather_2(kall, ksend, krecv)

    lane = lax.broadcasted_iota(jnp.int32, (1, DIM), 1)
    low = jnp.full((1, DIM), 2 * ALL_HEADS * SPAN, jnp.int32)
    high = jnp.zeros((1, DIM), jnp.int32)
    end = jnp.int32(0)
    for i in range(DOCS):
        low = jnp.where(lane == i, end, low)
        end = end + docs[i]
        high = jnp.where(lane == i, end, high)

    @pl.loop(0, 4 * PLANE)
    def _(block):
        at = block * ROWS + lax.broadcasted_iota(jnp.int32, (ROWS, 1), 0)
        tags[block] = ((at >= low) & (at < high)).astype(F32).astype(BF16)

    other = jnp.where((position >= low) & (position < high) | (lane >= DOCS), 0.0, FAR).astype(BF16)
    others = jnp.concatenate([other] * HEADS, axis=0)
    for h in range(HEADS):
        mtab[h] = jnp.full((ROWS, DIM), FAR, F32)
        dsum[h] = jnp.zeros((ROWS, DIM), F32)

    arrived(phase)
    state = jnp.zeros((SLICE, DIM), F32)
    for k in range(3):
        state = jnp.where(k < z, state * zbuf[k, SLICE : SLICE + 1] + zbuf[k, 0:SLICE], state)
    for k in range(PLANE):
        psend[k] = state * pfac[k, 0:1] + ppre[k]
    phase = start([
        remote(psend.at[lax.rem(spot + d, PLANE)], yin.at[spot], rsend, rrecv, d - 1, plane_peer(d))
        for d in range(1, PLANE)
    ])
    yin[spot] = psend[spot]
    for load in loads[5:]:
        load.wait()
    arrived(phase_k)
    arrived(phase)
    phase_k = [gather_3(kall, ksend, krecv, half) for half in (0, 1)]

    squares = jnp.zeros((ROWS, DIM), F32)
    for h in range(HEADS):
        cols = slice(h * DIM, (h + 1) * DIM)
        parts = halves(yin[2 * h : 2 * h + 2].reshape(DIM, DIM))
        carried = matmul(qb[:, cols], jnp.concatenate(parts, axis=1), 1, 0)
        weight = jnp.exp(cum_col[:, h : h + 1]) * continues
        attention = loc[:, cols] + weight * (carried[:, :DIM] + carried[:, DIM:])
        loc[:, cols] = attention
        squares = squares + attention * attention

    eye = row == col
    total = jnp.sum(squares, axis=1, keepdims=True)
    sqb[0] = jnp.broadcast_to(jnp.sum(jnp.where(eye, total, 0.0), axis=0, keepdims=True), (8, ROWS))
    phase = start([
        remote(sqb.at[0], sqb.at[i + 1], qsend, qrecv, i, quad[i]) for i in range(3)
    ])
    for h in range(HEADS):
        cols = slice(h * DIM, (h + 1) * DIM)
        gate = jax.nn.sigmoid(ogb[:, cols].astype(F32))
        loc[:, cols] = loc[:, cols] * (gb[:, cols] * gate)
    arrived(phase)
    total = sqb[0, 0:1] + sqb[1, 0:1] + (sqb[2, 0:1] + sqb[3, 0:1])
    total = jnp.sum(jnp.where(eye, total, 0.0), axis=1, keepdims=True)
    scale = lax.rsqrt(total / (ALL_HEADS * DIM) + EPSILON)
    for h in range(HEADS):
        cols = slice(h * DIM, (h + 1) * DIM)
        linb[:, cols] = (loc[:, cols] * scale).astype(BF16)
    vall[z, x, y] = matmul(linb[...], vpb[...], 1, 0).astype(BF16)
    phase_v = gather_1(vall, vsend, vrecv)

    lin_own = pltpu.make_async_copy(linb, out.at[0, :, columns], own_sem.at[len(PARTS)])

    @pl.when(p == 0)
    def _():
        lin_own.start()

    def probe(group, diagonal):
        over = group // 2
        wide = pl.ds(2 * lax.rem(group, 2), 2)
        keys = jnp.concatenate(
            [
                kall[over, wide].reshape(SPAN, DIM),
                tags[pl.ds(group * 8, 8)].reshape(SPAN, DIM),
            ],
            axis=1,
        )

        if True:
            asked = jnp.concatenate([qs[...].reshape(HEADS * ROWS, DIM), others], axis=1)
            raw = matmul(asked, keys, 1, 1)
            for h in range(HEADS):
                i = h
                scores = raw[i * ROWS : (i + 1) * ROWS]
                if diagonal:
                    at = group * SPAN + lax.broadcasted_iota(jnp.int32, (1, SPAN), 1)
                    scores = jnp.where(at <= position, scores, FAR)
                top = jnp.max(scores, axis=1, keepdims=True)
                prob = jnp.exp2((scores - top) * SLOPE)
                probs[group, h] = prob.astype(BF16)
                mtab[h] = jnp.where(lane == group, top, mtab[h])
                ltab[group, h] = sum(prob[:, k : k + DIM] for k in range(0, SPAN, DIM))

    whole = lax.div(ctx, 8)

    def nth(half, i):
        return lax.div(i, 2) * 4 + lax.rem(i, 2) + 2 * half

    def below(half, limit):
        return sum(lax.div(limit + 7 - nth(half, jnp.int32(i)), 8) for i in range(4))

    def probe_half(half, low, high):
        @pl.loop(low, high)
        def _(i):
            probe(nth(half, i), False)

    arrived(phase_v)
    phase_v = gather_2(vall, vsend, vrecv)
    lin_copy = remote(linb, out.at[0, :, columns], osend, orecv, 0, quad[0])

    @pl.when(p == 1)
    def _():
        lin_copy.start()

    arrived(phase_k[0])
    ready, some = below(0, whole), lax.div(below(0, whole), 2)
    probe_half(0, jnp.int32(0), some)
    arrived(phase_v)
    phase_v = [gather_3(vall, vsend, vrecv, half) for half in (0, 1)]
    probe_half(0, some, ready)
    arrived(phase_k[1])
    probe(whole, True)
    probe_half(1, jnp.int32(0), below(1, whole))

    for h in range(HEADS):
        table = mtab[h]
        top = jnp.max(table, axis=1, keepdims=True)
        mtab[h] = jnp.exp2((table - top) * SLOPE)

    def gathered(half, start_head, size, sums):
        def step(n, sums):
            group = nth(half, n)
            values = vall[group // 2, pl.ds(2 * lax.rem(group, 2), 2)].reshape(SPAN, DIM)
            heads = pl.ds(start_head, size)
            product = matmul(probs[group, heads].reshape(size * ROWS, SPAN), values, 1, 0)
            result = []
            for i in range(size):
                share = jnp.sum(jnp.where(lane == group, mtab[start_head + i], 0.0), axis=1, keepdims=True)
                dsum[start_head + i] += share * ltab[group, start_head + i]
                result.append(sums[i] + share * product[i * ROWS : (i + 1) * ROWS])
            return tuple(result)

        return lax.fori_loop(jnp.int32(0), below(half, whole + 1), step, sums)

    arrived(phase_v[0])
    sums = gathered(0, 0, HEADS, tuple(jnp.zeros((ROWS, DIM), F32) for _ in range(HEADS)))
    for h in range(HEADS):
        asum[h] = sums[h]
    arrived(phase_v[1])

    def share_of(part):
        low, size = PARTS[part]
        return softb.at[:, pl.ds(low * DIM, size * DIM)], out.at[
            0, :, pl.ds(pl.multiple_of(p * WIDTH + low * DIM, 2 * DIM), size * DIM)
        ]

    soft_copies = [
        remote(*share_of(part), osend, orecv, part + 1, quad[0]) for part in range(len(PARTS))
    ]
    soft_own = [
        pltpu.make_async_copy(*share_of(part), own_sem.at[part]) for part in range(len(PARTS))
    ]
    for team, (low, size) in enumerate(PARTS):
        sums = gathered(1, low, size, tuple(asum[low + i] for i in range(size)))
        for i in range(size):
            softb[:, (low + i) * DIM : (low + i + 1) * DIM] = (
                sums[i] / jnp.sum(dsum[low + i], axis=1, keepdims=True)
            ).astype(BF16)

        @pl.when(p == 0)
        def _():
            soft_copies[team].start()

        @pl.when(p == 1)
        def _():
            soft_own[team].start()

    for copies, sends, _ in started:
        only(sends, lambda copy: copy.wait_send(), copies)

    @pl.when(p == 0)
    def _():
        for copy in soft_copies:
            copy.wait_send()
        lin_copy.wait_recv()
        lin_own.wait()

    @pl.when(p == 1)
    def _():
        lin_copy.wait_send()
        for copy in soft_own:
            copy.wait()
        for copy in soft_copies:
            copy.wait_recv()


def local(lq, lk, lv, ld, og, gain, vp, sq, sk, docs):
    anywhere = pl.BlockSpec(memory_space=pl.ANY)
    vmem = pl.BlockSpec(memory_space=pltpu.VMEM)
    dma = lambda n: pltpu.SemaphoreType.DMA((n,))
    blocks = (4, 4, 4, ROWS, DIM)
    return pl.pallas_call(
        section_kernel,
        out_shape=jax.ShapeDtypeStruct((1, ROWS, 2 * WIDTH), BF16),
        in_specs=[anywhere] * 9 + [pl.BlockSpec(memory_space=pltpu.SMEM)],
        out_specs=anywhere,
        scratch_shapes=[
            pltpu.VMEM((ROWS, WIDTH), BF16),
            pltpu.VMEM((ROWS, WIDTH), BF16),
            pltpu.VMEM((ROWS, WIDTH), BF16),
            pltpu.VMEM((HEADS, ROWS), F32),
            pltpu.VMEM((ROWS, WIDTH), BF16),
            pltpu.VMEM((1, WIDTH), F32),
            pltpu.VMEM((WIDTH, DIM), BF16),
            pltpu.VMEM((HEADS, ROWS, DIM), BF16),
            pltpu.VMEM(blocks, BF16),
            pltpu.VMEM(blocks, BF16),
            pltpu.VMEM((4 * PLANE, ROWS, DIM), BF16),
            pltpu.VMEM((PLANE, SLICE + 8, DIM), F32),
            pltpu.VMEM((PLANE, SLICE + 8, DIM), F32),
            pltpu.VMEM((PLANE, SLICE, DIM), F32),
            pltpu.VMEM((PLANE, 8, DIM), F32),
            pltpu.VMEM((SLICE + 8, DIM), F32),
            pltpu.VMEM((4, SLICE + 8, DIM), F32),
            pltpu.VMEM((PLANE, SLICE, DIM), F32),
            pltpu.VMEM((PLANE, SLICE, DIM), F32),
            pltpu.VMEM((ROWS, WIDTH), F32),
            pltpu.VMEM((4, 8, ROWS), F32),
            pltpu.VMEM((ROWS, WIDTH), BF16),
            pltpu.VMEM((ROWS, WIDTH), BF16),
            pltpu.VMEM((GROUPS, HEADS, ROWS, SPAN), BF16),
            pltpu.VMEM((HEADS, ROWS, DIM), F32),
            pltpu.VMEM((GROUPS, HEADS, ROWS, DIM), F32),
            pltpu.VMEM((HEADS, ROWS, DIM), F32),
            pltpu.VMEM((HEADS, ROWS, DIM), F32),
            dma(8), dma(8), dma(27), dma(27), dma(27), dma(27), dma(15), dma(15), dma(3), dma(3),
            dma(15), dma(15), dma(3), dma(3), dma(1 + len(PARTS)), dma(1 + len(PARTS)), dma(1 + len(PARTS)),
        ],
        compiler_params=pltpu.CompilerParams(
            collective_id=0, has_side_effects=True, vmem_limit_bytes=60 << 20
        ),
        name="section",
    )(lq, lk, lv, ld, og, gain.reshape(1, -1), vp, sq, sk, docs)


def solution(mesh):
    return jax.shard_map(
        local,
        mesh=mesh,
        in_specs=(
            P("ctx", "tp"), P("ctx", "tp"), P("ctx", "tp"), P("tp", "ctx"), P("ctx", "tp"),
            P("tp"), P("tp", None, None), P("ctx", "tp"), P("ctx", "tp"), P(),
        ),
        out_specs=P("pipe", "ctx", "tp"),
        check_vma=False,
    )
```

```python
import math

import jax
import jax.numpy as jnp
from jax import lax
from jax.experimental import pallas as pl
from jax.experimental.pallas import tpu as pltpu
from jax.sharding import PartitionSpec as P

MESH = pl.DeviceIdType.MESH
ALL_HEADS = 32
DIM = 128
ROWS = 144
HEADS = 8
WIDTH = HEADS * DIM
PLANE = 16
SLICE = 64
SPAN = 8 * ROWS
GROUPS = 8
TEAM = 4
TEAMS = HEADS // TEAM
PARTS = ((0, 2), (2, 2), (4, 2), (6, 2))
FAR = -(2.0**100)
SLOPE = math.log2(math.e) / math.sqrt(DIM)
DOCS = 8
EPSILON = 1e-06
F32 = jnp.float32
BF16 = jnp.bfloat16


def place():
    ctx = lax.axis_index("ctx")
    return (
        lax.axis_index("pipe"),
        lax.div(ctx, 16),
        lax.rem(lax.div(ctx, 4), 4),
        lax.rem(ctx, 4),
        lax.axis_index("tp"),
    )


def doc_starts(docs, positions):
    end = jnp.int32(0)
    start = jnp.zeros_like(positions)
    for i in range(DOCS):
        end = end + docs[i]
        start = jnp.where(end <= positions, end, start)
    return start


def halves(x):
    high = x.astype(BF16)
    return high, (x - high.astype(F32)).astype(BF16)


def thirds(x):
    high = x.astype(BF16)
    rest = x - high.astype(F32)
    mid = rest.astype(BF16)
    return high, mid, (rest - mid.astype(F32)).astype(BF16)


def matmul(a, b, ca, cb):
    return lax.dot_general(a, b, (((ca,), (cb,)), ((), ())), preferred_element_type=F32)


def section_kernel(
    lq, lk, lv, ld, og, gain, vp, sq, sk, docs,
    out,
    qb, kb, vb, ldb, ogb, gb, vpb, qs, kall, vall, tags,
    bst, pbuf, ppre, pfac, zsend, zbuf, psend, yin,
    loc, sqb, linb, softb, probs, mtab, ltab, dsum, asum,
    load_sem, qload_sem, ksend, krecv, vsend, vrecv, ssend, srecv, zs, zr, rsend, rrecv, qsend, qrecv, osend, orecv, own_sem,
):
    p, z, x, y, t = place()
    spot = x * 4 + y
    ctx = z * PLANE + spot
    first = ctx * ROWS

    columns = pl.ds(pl.multiple_of(p * WIDTH, WIDTH), WIDTH)
    loads = [
        pltpu.make_async_copy(src, dst, load_sem.at[i])
        for i, (src, dst) in enumerate((
            (sk.at[:, pl.ds(pl.multiple_of(p * DIM, DIM), DIM)], kall.at[z, x, y]),
            (ld.at[pl.ds(pl.multiple_of(p * HEADS, HEADS), HEADS)], ldb),
            (lk.at[:, columns], kb),
            (lv.at[:, columns], vb),
            (lq.at[:, columns], qb),
            (og.at[:, columns], ogb),
            (gain.at[:, columns], gb),
            (vp.at[p], vpb),
        ))
    ]
    loads += [
        pltpu.make_async_copy(
            sq.at[:, pl.ds(pl.multiple_of(p * WIDTH + h * DIM, DIM), DIM)], qs.at[h], qload_sem.at[h]
        )
        for h in range(HEADS)
    ]

    def plane_peer(d):
        return (p, z * PLANE + lax.rem(spot + d, PLANE), t)

    def y_peer(d):
        return (p, z * PLANE + x * 4 + lax.rem(y + d, 4), t)

    def x_peer(d):
        return (p, z * PLANE + lax.rem(x + d, 4) * 4 + y, t)

    def z_peer(d):
        return (p, lax.rem(z + d, 4) * PLANE + spot, t)

    quad = [(1 - p, ctx, t), (p, ctx, 1 - t), (1 - p, ctx, 1 - t)]

    barrier = pltpu.get_barrier_semaphore()
    for peer in [plane_peer(d) for d in range(1, PLANE)] + [z_peer(d) for d in (1, 2, 3)] + quad:
        pl.semaphore_signal(barrier, inc=1, device_id=peer, device_id_type=MESH)
    for load in loads:
        load.start()

    row = lax.broadcasted_iota(jnp.int32, (ROWS, ROWS), 0)
    col = lax.broadcasted_iota(jnp.int32, (ROWS, ROWS), 1)
    position = first + lax.broadcasted_iota(jnp.int32, (ROWS, 1), 0)
    begin = doc_starts(docs, position) - first
    last_begin = doc_starts(docs, jnp.full((1, 1), first + ROWS - 1, jnp.int32)) - first
    lower = (row >= col).astype(F32).astype(BF16)
    same_doc = (row >= col) & (col >= begin)
    continues = (begin < 0).astype(F32)
    last_continues = (last_begin < 0).astype(F32)
    in_last = (lax.broadcasted_iota(jnp.int32, (ROWS, 1), 0) >= last_begin).astype(F32)

    loads[0].wait()
    pl.semaphore_wait(barrier, PLANE - 1 + 6)

    def remote(src, dst, send, recv, i, peer):
        return pltpu.make_async_remote_copy(
            src_ref=src, dst_ref=dst, send_sem=send.at[i], recv_sem=recv.at[i],
            device_id=peer, device_id_type=MESH,
        )

    started = []

    def only(condition, act, copies):
        def all_of_them():
            for copy in copies:
                act(copy)

        if condition is None:
            all_of_them()
        else:
            pl.when(condition)(all_of_them)

    def start_bundles(bundles):
        for copies, sends, _ in bundles:
            only(sends, lambda copy: copy.start(), copies)
        started.extend(bundles)
        return bundles

    def start(copies):
        return start_bundles([(copies, None, None)])

    def arrived(bundles):
        for copies, _, receives in bundles:
            only(receives, lambda copy: copy.wait_recv(), copies)

    def upto(layer):
        return None if layer == 0 else z >= layer

    def gather_1(buf, send, recv):
        mine = buf.at[z, x, y]
        return start_bundles([
            ([remote(mine, mine, send, recv, d - 1, z_peer(d))], z + d < 4, z >= d) for d in (1, 2, 3)
        ])

    def gather_2(buf, send, recv):
        bundles = []
        for layer in range(4):
            mine, peer = buf.at[layer, x, y], x_peer if layer < 2 else y_peer
            copies = [remote(mine, mine, send, recv, 3 * layer + d + 2, peer(d)) for d in (1, 2, 3)]
            bundles.append((copies, upto(layer), upto(layer)))
        return start_bundles(bundles)

    def gather_3(buf, send, recv, half):
        a, b = buf.at[half, :, y], buf.at[half + 2, x]
        via_y = [remote(a, a, send, recv, d + 14 + 6 * half, y_peer(d)) for d in (1, 2, 3)]
        via_x = [remote(b, b, send, recv, d + 17 + 6 * half, x_peer(d)) for d in (1, 2, 3)]
        return start_bundles([
            (via_y, upto(half), upto(half)), (via_x, upto(half + 2), upto(half + 2)),
        ])

    phase_k = gather_1(kall, ksend, krecv)

    loads[1].wait()
    pieces = thirds(ldb[...])
    cum_row = sum(matmul(a, lower, 1, 1) for a in pieces)
    cum_col = sum(matmul(lower, a, 1, 1) for a in pieces)

    loads[2].wait()
    loads[3].wait()
    for h in range(HEADS):
        cols = slice(h * DIM, (h + 1) * DIM)
        last = cum_row[h : h + 1, ROWS - 1 : ROWS]
        tail = jnp.exp(last - cum_col[:, h : h + 1]) * in_last
        parts = halves(vb[:, cols].astype(F32) * tail)
        state = matmul(kb[:, cols], jnp.concatenate(parts, axis=1), 0, 0)
        state = state[:, :DIM] + state[:, DIM:]
        factor = jnp.broadcast_to(jnp.exp(last) * last_continues, (8, DIM))
        for i in range(2):
            bst[2 * h + i, 0:SLICE] = state[i * SLICE : (i + 1) * SLICE]
            bst[2 * h + i, SLICE : SLICE + 8] = factor

    phase = start([
        remote(bst.at[lax.rem(spot + d, PLANE)], pbuf.at[spot], ssend, srecv, d - 1, plane_peer(d))
        for d in range(1, PLANE)
    ])
    pbuf[spot] = bst[spot]

    loads[4].wait()
    for h in range(HEADS):
        cols = slice(h * DIM, (h + 1) * DIM)
        scores = matmul(qb[:, cols], kb[:, cols], 1, 1)
        gap = jnp.minimum(cum_col[:, h : h + 1] - cum_row[h : h + 1, :], 0.0)
        weights = (scores * jnp.where(same_doc, jnp.exp(gap), 0.0)).astype(BF16)
        loc[:, cols] = matmul(weights, vb[:, cols], 1, 0)

    arrived(phase)
    prefix = jnp.zeros((SLICE, DIM), F32)
    factor = jnp.ones((8, DIM), F32)
    for k in range(PLANE):
        ppre[k] = prefix
        pfac[k] = factor
        f = pbuf[k, SLICE : SLICE + 8]
        prefix = prefix * f[0:1] + pbuf[k, 0:SLICE]
        factor = factor * f
    zsend[0:SLICE] = prefix
    zsend[SLICE : SLICE + 8] = factor
    phase = start([remote(zsend, zbuf.at[z], zs, zr, d - 1, z_peer(d)) for d in (1, 2, 3)])
    zbuf[z] = zsend[...]

    arrived(phase_k)
    phase_k = gather_2(kall, ksend, krecv)

    lane = lax.broadcasted_iota(jnp.int32, (1, DIM), 1)
    low = jnp.full((1, DIM), 2 * ALL_HEADS * SPAN, jnp.int32)
    high = jnp.zeros((1, DIM), jnp.int32)
    end = jnp.int32(0)
    for i in range(DOCS):
        low = jnp.where(lane == i, end, low)
        end = end + docs[i]
        high = jnp.where(lane == i, end, high)

    @pl.loop(0, 4 * PLANE)
    def _(block):
        at = block * ROWS + lax.broadcasted_iota(jnp.int32, (ROWS, 1), 0)
        tags[block] = ((at >= low) & (at < high)).astype(F32).astype(BF16)

    other = jnp.where((position >= low) & (position < high) | (lane >= DOCS), 0.0, FAR).astype(BF16)
    others = jnp.concatenate([other] * HEADS, axis=0)
    for h in range(HEADS):
        mtab[h] = jnp.full((ROWS, DIM), FAR, F32)
        dsum[h] = jnp.zeros((ROWS, DIM), F32)

    arrived(phase)
    state = jnp.zeros((SLICE, DIM), F32)
    for k in range(3):
        state = jnp.where(k < z, state * zbuf[k, SLICE : SLICE + 1] + zbuf[k, 0:SLICE], state)
    for k in range(PLANE):
        psend[k] = state * pfac[k, 0:1] + ppre[k]
    phase = start([
        remote(psend.at[lax.rem(spot + d, PLANE)], yin.at[spot], rsend, rrecv, d - 1, plane_peer(d))
        for d in range(1, PLANE)
    ])
    yin[spot] = psend[spot]
    for load in loads[5:]:
        load.wait()
    arrived(phase_k)
    arrived(phase)
    phase_k = [gather_3(kall, ksend, krecv, half) for half in (0, 1)]

    squares = jnp.zeros((ROWS, DIM), F32)
    for h in range(HEADS):
        cols = slice(h * DIM, (h + 1) * DIM)
        parts = halves(yin[2 * h : 2 * h + 2].reshape(DIM, DIM))
        carried = matmul(qb[:, cols], jnp.concatenate(parts, axis=1), 1, 0)
        weight = jnp.exp(cum_col[:, h : h + 1]) * continues
        attention = loc[:, cols] + weight * (carried[:, :DIM] + carried[:, DIM:])
        loc[:, cols] = attention
        squares = squares + attention * attention

    eye = row == col
    total = jnp.sum(squares, axis=1, keepdims=True)
    sqb[0] = jnp.broadcast_to(jnp.sum(jnp.where(eye, total, 0.0), axis=0, keepdims=True), (8, ROWS))
    phase = start([
        remote(sqb.at[0], sqb.at[i + 1], qsend, qrecv, i, quad[i]) for i in range(3)
    ])
    for h in range(HEADS):
        cols = slice(h * DIM, (h + 1) * DIM)
        gate = jax.nn.sigmoid(ogb[:, cols].astype(F32))
        loc[:, cols] = loc[:, cols] * (gb[:, cols] * gate)
    arrived(phase)
    total = sqb[0, 0:1] + sqb[1, 0:1] + (sqb[2, 0:1] + sqb[3, 0:1])
    total = jnp.sum(jnp.where(eye, total, 0.0), axis=1, keepdims=True)
    scale = lax.rsqrt(total / (ALL_HEADS * DIM) + EPSILON)
    for h in range(HEADS):
        cols = slice(h * DIM, (h + 1) * DIM)
        linb[:, cols] = (loc[:, cols] * scale).astype(BF16)
    vall[z, x, y] = matmul(linb[...], vpb[...], 1, 0).astype(BF16)
    phase_v = gather_1(vall, vsend, vrecv)

    lin_own = pltpu.make_async_copy(linb, out.at[0, :, columns], own_sem.at[len(PARTS)])

    @pl.when(p == 0)
    def _():
        lin_own.start()

    def probe(group, diagonal):
        over = group // 2
        wide = pl.ds(2 * lax.rem(group, 2), 2)
        keys = jnp.concatenate(
            [
                kall[over, wide].reshape(SPAN, DIM),
                tags[pl.ds(group * 8, 8)].reshape(SPAN, DIM),
            ],
            axis=1,
        )

        if True:
            asked = jnp.concatenate([qs[...].reshape(HEADS * ROWS, DIM), others], axis=1)
            raw = matmul(asked, keys, 1, 1)
            for h in range(HEADS):
                i = h
                scores = raw[i * ROWS : (i + 1) * ROWS]
                if diagonal:
                    at = group * SPAN + lax.broadcasted_iota(jnp.int32, (1, SPAN), 1)
                    scores = jnp.where(at <= position, scores, FAR)
                top = jnp.max(scores, axis=1, keepdims=True)
                prob = jnp.exp2((scores - top) * SLOPE)
                probs[group, h] = prob.astype(BF16)
                mtab[h] = jnp.where(lane == group, top, mtab[h])
                ltab[group, h] = sum(prob[:, k : k + DIM] for k in range(0, SPAN, DIM))

    whole = lax.div(ctx, 8)

    def nth(half, i):
        return lax.div(i, 2) * 4 + lax.rem(i, 2) + 2 * half

    def below(half, limit):
        return sum(lax.div(limit + 7 - nth(half, jnp.int32(i)), 8) for i in range(4))

    def probe_half(half, low, high):
        @pl.loop(low, high)
        def _(i):
            probe(nth(half, i), False)

    arrived(phase_v)
    phase_v = gather_2(vall, vsend, vrecv)
    lin_copy = remote(linb, out.at[0, :, columns], osend, orecv, 0, quad[0])

    @pl.when(p == 1)
    def _():
        lin_copy.start()

    arrived(phase_k[0])
    ready, some = below(0, whole), lax.div(below(0, whole), 2)
    probe_half(0, jnp.int32(0), some)
    arrived(phase_v)
    phase_v = [gather_3(vall, vsend, vrecv, half) for half in (0, 1)]
    probe_half(0, some, ready)
    arrived(phase_k[1])
    probe(whole, True)
    probe_half(1, jnp.int32(0), below(1, whole))

    for h in range(HEADS):
        table = mtab[h]
        top = jnp.max(table, axis=1, keepdims=True)
        mtab[h] = jnp.exp2((table - top) * SLOPE)

    def gathered(half, start_head, size, sums):
        def step(n, sums):
            group = nth(half, n)
            values = vall[group // 2, pl.ds(2 * lax.rem(group, 2), 2)].reshape(SPAN, DIM)
            heads = pl.ds(start_head, size)
            product = matmul(probs[group, heads].reshape(size * ROWS, SPAN), values, 1, 0)
            result = []
            for i in range(size):
                share = jnp.sum(jnp.where(lane == group, mtab[start_head + i], 0.0), axis=1, keepdims=True)
                dsum[start_head + i] += share * ltab[group, start_head + i]
                result.append(sums[i] + share * product[i * ROWS : (i + 1) * ROWS])
            return tuple(result)

        return lax.fori_loop(jnp.int32(0), below(half, whole + 1), step, sums)

    arrived(phase_v[0])
    sums = gathered(0, 0, HEADS, tuple(jnp.zeros((ROWS, DIM), F32) for _ in range(HEADS)))
    for h in range(HEADS):
        asum[h] = sums[h]
    arrived(phase_v[1])

    def share_of(part):
        low, size = PARTS[part]
        return softb.at[:, pl.ds(low * DIM, size * DIM)], out.at[
            0, :, pl.ds(pl.multiple_of(p * WIDTH + low * DIM, 2 * DIM), size * DIM)
        ]

    soft_copies = [
        remote(*share_of(part), osend, orecv, part + 1, quad[0]) for part in range(len(PARTS))
    ]
    soft_own = [
        pltpu.make_async_copy(*share_of(part), own_sem.at[part]) for part in range(len(PARTS))
    ]
    for team, (low, size) in enumerate(PARTS):
        sums = gathered(1, low, size, tuple(asum[low + i] for i in range(size)))
        for i in range(size):
            softb[:, (low + i) * DIM : (low + i + 1) * DIM] = (
                sums[i] / jnp.sum(dsum[low + i], axis=1, keepdims=True)
            ).astype(BF16)

        @pl.when(p == 0)
        def _():
            soft_copies[team].start()

        @pl.when(p == 1)
        def _():
            soft_own[team].start()

    for copies, sends, _ in started:
        only(sends, lambda copy: copy.wait_send(), copies)

    @pl.when(p == 0)
    def _():
        for copy in soft_copies:
            copy.wait_send()
        lin_copy.wait_recv()
        lin_own.wait()

    @pl.when(p == 1)
    def _():
        lin_copy.wait_send()
        for copy in soft_own:
            copy.wait()
        for copy in soft_copies:
            copy.wait_recv()


def local(lq, lk, lv, ld, og, gain, vp, sq, sk, docs):
    anywhere = pl.BlockSpec(memory_space=pl.ANY)
    vmem = pl.BlockSpec(memory_space=pltpu.VMEM)
    dma = lambda n: pltpu.SemaphoreType.DMA((n,))
    blocks = (4, 4, 4, ROWS, DIM)
    return pl.pallas_call(
        section_kernel,
        out_shape=jax.ShapeDtypeStruct((1, ROWS, 2 * WIDTH), BF16),
        in_specs=[anywhere] * 9 + [pl.BlockSpec(memory_space=pltpu.SMEM)],
        out_specs=anywhere,
        scratch_shapes=[
            pltpu.VMEM((ROWS, WIDTH), BF16),
            pltpu.VMEM((ROWS, WIDTH), BF16),
            pltpu.VMEM((ROWS, WIDTH), BF16),
            pltpu.VMEM((HEADS, ROWS), F32),
            pltpu.VMEM((ROWS, WIDTH), BF16),
            pltpu.VMEM((1, WIDTH), F32),
            pltpu.VMEM((WIDTH, DIM), BF16),
            pltpu.VMEM((HEADS, ROWS, DIM), BF16),
            pltpu.VMEM(blocks, BF16),
            pltpu.VMEM(blocks, BF16),
            pltpu.VMEM((4 * PLANE, ROWS, DIM), BF16),
            pltpu.VMEM((PLANE, SLICE + 8, DIM), F32),
            pltpu.VMEM((PLANE, SLICE + 8, DIM), F32),
            pltpu.VMEM((PLANE, SLICE, DIM), F32),
            pltpu.VMEM((PLANE, 8, DIM), F32),
            pltpu.VMEM((SLICE + 8, DIM), F32),
            pltpu.VMEM((4, SLICE + 8, DIM), F32),
            pltpu.VMEM((PLANE, SLICE, DIM), F32),
            pltpu.VMEM((PLANE, SLICE, DIM), F32),
            pltpu.VMEM((ROWS, WIDTH), F32),
            pltpu.VMEM((4, 8, ROWS), F32),
            pltpu.VMEM((ROWS, WIDTH), BF16),
            pltpu.VMEM((ROWS, WIDTH), BF16),
            pltpu.VMEM((GROUPS, HEADS, ROWS, SPAN), BF16),
            pltpu.VMEM((HEADS, ROWS, DIM), F32),
            pltpu.VMEM((GROUPS, HEADS, ROWS, DIM), F32),
            pltpu.VMEM((HEADS, ROWS, DIM), F32),
            pltpu.VMEM((HEADS, ROWS, DIM), F32),
            dma(8), dma(8), dma(27), dma(27), dma(27), dma(27), dma(15), dma(15), dma(3), dma(3),
            dma(15), dma(15), dma(3), dma(3), dma(1 + len(PARTS)), dma(1 + len(PARTS)), dma(1 + len(PARTS)),
        ],
        compiler_params=pltpu.CompilerParams(
            collective_id=0, has_side_effects=True, vmem_limit_bytes=60 << 20
        ),
        name="section",
    )(lq, lk, lv, ld, og, gain.reshape(1, -1), vp, sq, sk, docs)


def solution(mesh):
    return jax.shard_map(
        local,
        mesh=mesh,
        in_specs=(
            P("ctx", "tp"), P("ctx", "tp"), P("ctx", "tp"), P("tp", "ctx"), P("ctx", "tp"),
            P("tp"), P("tp", None, None), P("ctx", "tp"), P("ctx", "tp"), P(),
        ),
        out_specs=P("pipe", "ctx", "tp"),
        check_vma=False,
    )
```
